256 devices in a mesh: sec: 4 (over x_hi, core), dev: 64 (over x_lo, y, z).
Axes of the slice: x: 4 (x_hi: 2, x_lo: 2; x = x_hi * 2 + x_lo), y: 4, z: 8, core: 2. Of those that a mesh axis runs over, the one named last changes fastest.
Arguments:
- feature_store: bfloat16 [1048576, 128], P(('sec', 'dev')), may hold values from -6 to 6
- send_rows: int32 [16384, 64], P(('sec', 'dev')), may hold values from 0 to 4095
- send_counts: int32 [16384], P(('sec', 'dev')), may hold values from 1 to 64, as said below
- target_one: int32 [131072], P(('sec', 'dev')), may hold values from 0 to 4095, as said below
- neighbor_one: int32 [15, 131072], P(None, ('sec', 'dev')), may hold values from 0 to 4095, as said below
- degree_one: int32 [131072], P(('sec', 'dev')), may hold values from 1 to 15
- target_two: int32 [32768], P(('sec', 'dev')), may hold values from 0 to 511
- neighbor_two: int32 [10, 32768], P(None, ('sec', 'dev')), may hold values from 0 to 511
- degree_two: int32 [32768], P(('sec', 'dev')), may hold values from 1 to 10
- weight_one: bfloat16 [256, 1024], replicated, may hold values from -0.375 to 0.375
- weight_two: bfloat16 [2048, 1024], replicated, may hold values from -0.125 to 0.125
- cotangent: bfloat16 [32768, 1024], P(('sec', 'dev')), may hold values from -0.125 to 0.125
Outputs:
- hidden_two: bfloat16 [32768, 1024], P(('sec', 'dev'))
- grad_one: float32 [1024, 256], P('dev')
- grad_two: float32 [1024, 2048], P('dev')
The draws below stay inside these ranges and needn't reach their ends.
Inputs may be any that keep to these rules, and one draw needn't show every extreme that they name: `send_counts`: in each section one trainer receives 64 filled slots from every store shard. `target_one`: each entry names a slot of received(b) that its store shard filled. `neighbor_one`: each entry names a slot of received(b) that its store shard filled.
All inputs are finite; a program needn't handle non-finite values.
Results may differ from the reference program's by a relative error of at most 0.0056.
Values may be sent and summed in bfloat16 or wider, within the bound.
No kernel may reach another device: no remote copies, remote signals or barrier semaphores. Data moves between devices by JAX's collectives and lax.ppermute only.
A program may use at most 64 MiB of HBM per device.

```python
import jax
import jax.numpy as jnp
from jax import lax

F = 128
H = 1024
FAN1 = 15
FAN2 = 10
CAP = 64
STORE_ROWS = 4096
M2 = 128
M1 = 512
N_SEC = 4
N_DEV = 64
DEVICES = 256


def store_layout(key):
    folded = jax.random.fold_in(key, 11)
    key_level, key_fill, key_busy = jax.random.split(folded, 3)
    load_level = jax.random.randint(key_level, (N_SEC, 1, N_DEV), 1, 5)
    lower_bound = CAP * load_level // 8 + 1
    upper_bound = CAP * load_level // 4 + 1
    spread = jax.random.randint(key_fill, (N_SEC, N_DEV, N_DEV), 0, 1 << 20)
    counts = lower_bound + spread % (upper_bound - lower_bound)
    busiest = jax.random.randint(key_busy, (N_SEC, 1, 1), 0, N_DEV)
    column = lax.broadcasted_iota(jnp.int32, (N_SEC, N_DEV, N_DEV), 2)
    return (jnp.where(column == busiest, CAP, counts).astype(jnp.int32), busiest)


def live_slots(key, salt_value, length):
    folded = jax.random.fold_in(key, salt_value)
    key_peer, key_slot = jax.random.split(folded)
    count_table, busiest = store_layout(key)
    counts = jnp.transpose(count_table, (0, 2, 1))
    peer_index = jax.random.randint(key_peer, (N_SEC, N_DEV, length), 0, N_DEV)
    chosen = jnp.take_along_axis(counts, peer_index, axis=2)
    spread = jax.random.randint(key_slot, (N_SEC, N_DEV, length), 0, 1 << 20)
    slots_drawn = peer_index * CAP + spread % chosen
    trainer = lax.broadcasted_iota(jnp.int32, (N_SEC, N_DEV, length), 1)
    position = lax.broadcasted_iota(jnp.int32, (N_SEC, N_DEV, length), 2)
    topmost = (trainer == busiest) & (position == 0)
    return jnp.where(topmost, N_DEV * CAP - 1, slots_drawn).astype(jnp.int32)


def degree_table(key, salt_value, fanout, length):
    folded = jax.random.fold_in(key, salt_value)
    key_degree, key_peak = jax.random.split(folded)
    values = jax.random.randint(key_degree, (length,), 1, fanout + 1)
    peak_index = jax.random.randint(key_peak, (), 0, length)
    return values.at[peak_index].set(fanout).astype(jnp.int32)


def draw_send_counts(key, part):
    return store_layout(key)[0].reshape(-1)


def draw_target_one(key, part):
    return live_slots(key, 21, M1).reshape(-1)


def draw_neighbor_one(key, part):
    slots_drawn = live_slots(key, 22, FAN1 * M1).reshape(N_SEC, N_DEV, FAN1, M1)
    return jnp.transpose(slots_drawn, (2, 0, 1, 3)).reshape(FAN1, N_SEC * N_DEV * M1)


def draw_degree_one(key, part):
    return degree_table(key, 31, FAN1, DEVICES * M1)


def draw_degree_two(key, part):
    return degree_table(key, 32, FAN2, DEVICES * M2)


def touch_ends(values, rng, smallest, high):
    place = [jax.random.randint(jax.random.fold_in(rng, axis), (), 0, length) for axis, length in enumerate(values.shape)]
    longest = values.shape.index(max(values.shape))
    neighbour = place[:longest] + [(place[longest] + 1) % values.shape[longest]] + place[longest + 1:]
    return values.at[tuple(place)].set(smallest).at[tuple(neighbour)].set(high)


def strengthened(drawn, key, source, target, parts, factor):
    def block_of(dim):
        return (jnp.arange(drawn.shape[dim]) // (drawn.shape[dim] // parts)).reshape((-1,) + (1,) * (drawn.ndim - 1 - dim))

    near = jax.random.permutation(key, parts)[block_of(target)]
    far = (block_of(target) + parts // 2) % parts
    return jnp.where((block_of(source) == near) | (block_of(source) == far), factor * drawn, drawn)


def steps_of(stream_key, shape, cuts, least, largest):
    def one(dim, shards_of):
        steps = jax.random.uniform(jax.random.fold_in(jax.random.fold_in(stream_key, 6), dim), (shards_of,), jnp.float32, least / len(cuts), largest / len(cuts))
        return jnp.repeat(jnp.exp(steps), shape[dim] // shards_of).reshape((-1,) + (1,) * (len(shape) - dim - 1))

    gain = one(*cuts[0])
    for cut in cuts[1:]:
        gain = gain * one(*cut)
    return gain


def noise(key, extent, width, bound, pieces=(), held_as=jnp.bfloat16):
    drawn = jax.random.normal(key, extent, jnp.float32) * width
    if len(pieces) > 0:
        drawn = steps_of(key, extent, pieces, -0.22, 0.18) * drawn
    return jnp.clip(drawn, min=-bound, max=bound).astype(held_as)


def gaussian_with(key, shape, scale, most, cuts, heavy, held_as=jnp.bfloat16):
    drawn = scale * jax.random.normal(key, shape, jnp.float32)
    if cuts:
        drawn = drawn * steps_of(key, shape, cuts, -0.22, 0.18)
    return jnp.clip(strengthened(drawn, jax.random.fold_in(key, 3), *heavy), -most, most).astype(held_as)


def setup_inputs(seed: int = 0) -> dict:
    seeds = jax.random.split(jax.random.key(seed), 13)
    return {
        "feature_store": noise(seeds[0], (DEVICES * STORE_ROWS, F), 1.0, 6.0, ((0, 256),)),
        "send_rows": touch_ends(jax.random.randint(seeds[1], (DEVICES * N_DEV, CAP), 0, STORE_ROWS), jax.random.fold_in(seeds[1], 1), 0, STORE_ROWS - 1).astype(jnp.int32),
        "send_counts": draw_send_counts(jax.random.fold_in(seeds[12], 71), 0),
        "target_one": draw_target_one(jax.random.fold_in(seeds[12], 71), 0),
        "neighbor_one": draw_neighbor_one(jax.random.fold_in(seeds[12], 71), 0),
        "degree_one": draw_degree_one(jax.random.fold_in(seeds[12], 71), 0),
        "target_two": touch_ends(jax.random.randint(seeds[6], (DEVICES * M2,), 0, M1), jax.random.fold_in(seeds[6], 1), 0, M1 - 1).astype(jnp.int32),
        "neighbor_two": touch_ends(jax.random.randint(seeds[7], (FAN2, DEVICES * M2), 0, M1), jax.random.fold_in(seeds[7], 1), 0, M1 - 1).astype(jnp.int32),
        "degree_two": draw_degree_two(jax.random.fold_in(seeds[12], 71), 0),
        "weight_one": noise(seeds[9], (2 * F, H), (2 * F) ** -0.5, 0.375),
        "weight_two": noise(seeds[10], (2 * H, H), (2 * H) ** -0.5, 0.125),
        "cotangent": gaussian_with(seeds[11], (DEVICES * M2, H), (M2 * DEVICES) ** -0.5, 0.125, ((0, 256),), (0, 1, 256, 6.0)),
    }


def activate(preact):
    return jnp.where(preact > 0, preact, jnp.expm1(jnp.minimum(preact, 0.0)))


def activate_slope(preact):
    return jnp.where(preact > 0, 1.0, jnp.exp(jnp.minimum(preact, 0.0)))


def mean_rows(source, neighbors, degrees):
    gathered = jnp.take(source, neighbors, axis=0)
    filled = lax.broadcasted_iota(jnp.int32, neighbors.shape, 0) < degrees[None, :]
    summed = jnp.sum(jnp.where(filled[:, :, None], gathered.astype(jnp.float32), 0.0), axis=0)
    return (summed / degrees.astype(jnp.float32)[:, None]).astype(jnp.bfloat16)


def sage_forward(source, targets, neighbors, degrees, weight):
    target_rows = jnp.take(source, targets, axis=0)
    averaged = mean_rows(source, neighbors, degrees)
    joined = jnp.concatenate([target_rows, averaged], axis=1)
    preact = jnp.dot(joined, weight, preferred_element_type=jnp.float32)
    return joined, preact, activate(preact).astype(jnp.bfloat16)


def spread_back(grad_joined, targets, neighbors, degrees, source_count):
    half_width = grad_joined.shape[1] // 2
    target_grad = grad_joined[:, :half_width].astype(jnp.float32)
    average_grad = grad_joined[:, half_width:].astype(jnp.float32) / degrees.astype(jnp.float32)[:, None]
    filled = lax.broadcasted_iota(jnp.int32, neighbors.shape, 0) < degrees[None, :]
    scaled = jnp.where(filled[:, :, None], average_grad[None], 0.0)
    summed_back = jnp.zeros((source_count, half_width), jnp.float32).at[targets].add(target_grad)
    summed_back = summed_back.at[neighbors.reshape(-1)].add(scaled.reshape(-1, half_width))
    return summed_back.astype(jnp.bfloat16)


def reference(feature_store, send_rows, send_counts, target_one, neighbor_one, degree_one, target_two, neighbor_two, degree_two, weight_one, weight_two, cotangent):
    feature_width = feature_store.shape[1]
    hidden_width = weight_two.shape[1]
    store_shards = feature_store.reshape(N_SEC, N_DEV, STORE_ROWS, feature_width)
    send_table = send_rows.reshape(N_SEC, N_DEV, N_DEV, CAP)
    fill_table = send_counts.reshape(N_SEC, N_DEV, N_DEV)

    def batched(array, length):
        return array.reshape(N_SEC, N_DEV, length)

    def batched_wide(array, fanout, length):
        return jnp.transpose(array.reshape(fanout, N_SEC, N_DEV, length), (1, 2, 0, 3))

    def next_section(array):
        moved = jnp.roll(array, -1, axis=0)
        return moved.reshape((N_SEC * N_DEV,) + moved.shape[2:])

    def flatten(array):
        return array.reshape((N_SEC * N_DEV,) + array.shape[2:])

    records = (jnp.arange(N_SEC * N_DEV, dtype=jnp.int32),
               flatten(batched(target_one, M1)), flatten(batched_wide(neighbor_one, FAN1, M1)), flatten(batched(degree_one, M1)),
               next_section(batched(target_two, M2)), next_section(batched_wide(neighbor_two, FAN2, M2)), next_section(batched(degree_two, M2)),
               next_section(cotangent.reshape(N_SEC, N_DEV, M2, hidden_width)))

    def advance(running, record):
        batch_index, target_first, neighbor_first, degree_first, target_second, neighbor_second, degree_second, upstream = record
        section = batch_index // N_DEV
        member = batch_index % N_DEV
        shards = store_shards[section]
        chosen_rows = send_table[section][:, member]
        live_count = fill_table[section][:, member]
        fetched = jax.vmap(lambda shard_rows, wanted: jnp.take(shard_rows, wanted, axis=0))(shards, chosen_rows)
        filled = lax.broadcasted_iota(jnp.int32, chosen_rows.shape, 1) < live_count[:, None]
        received = jnp.where(filled[:, :, None], fetched, jnp.zeros((), fetched.dtype)).reshape(N_DEV * CAP, feature_width)
        joined_one, pre_one, hidden_one = sage_forward(received, target_first, neighbor_first, degree_first, weight_one)
        joined_two, pre_two, hidden_two = sage_forward(hidden_one, target_second, neighbor_second, degree_second, weight_two)
        grad_pre_two = (upstream.astype(jnp.float32) * activate_slope(pre_two)).astype(jnp.bfloat16)
        grad_joined_two = jnp.dot(grad_pre_two, weight_two.T, preferred_element_type=jnp.float32).astype(jnp.bfloat16)
        grad_hidden = spread_back(grad_joined_two, target_second, neighbor_second, degree_second, M1)
        grad_pre_one = (grad_hidden.astype(jnp.float32) * activate_slope(pre_one)).astype(jnp.bfloat16)
        grad_one = running[0] + jnp.dot(grad_pre_one.T, joined_one, preferred_element_type=jnp.float32)
        grad_two = running[1] + jnp.dot(grad_pre_two.T, joined_two, preferred_element_type=jnp.float32)
        return (grad_one, grad_two), hidden_two

    initial = (jnp.zeros((hidden_width, 2 * feature_width), jnp.float32), jnp.zeros((hidden_width, 2 * hidden_width), jnp.float32))
    sums_final, outputs = lax.scan(advance, initial, records)
    placed = jnp.roll(outputs.reshape(N_SEC, N_DEV, M2, hidden_width), 1, axis=0)
    return placed.reshape(N_SEC * N_DEV * M2, hidden_width), sums_final[0], sums_final[1]
```

```python
import functools

import jax
import jax.numpy as jnp
from jax import lax
from jax.experimental import pallas as pl
from jax.experimental.pallas import tpu as pltpu
from jax.sharding import Mesh, PartitionSpec as P


F = 128
H = 1024
FAN1 = 15
FAN2 = 10
CAP = 64
STORE_ROWS = 4096
M2 = 128
M1 = 512
PEERS = 64
TABLE = PEERS * CAP
AXES = ("xh", "core", "xl", "y", "z")
SEC = ("xh", "core")
DEV = ("xl", "y", "z")
PLANE = ("xh", "xl", "y")

bf16 = jnp.bfloat16
f32 = jnp.float32
VMEM = pl.BlockSpec(memory_space=pltpu.VMEM)
SMEM = pl.BlockSpec(memory_space=pltpu.SMEM)
LIMIT = pltpu.CompilerParams(vmem_limit_bytes=56 * 1024 * 1024)


def shape(dims, dtype):
    return jax.ShapeDtypeStruct(dims, dtype)


def widen(source, wide, rows):
    def chunk(step, carry):
        here = pl.ds(pl.multiple_of(step * 256, 256), 256)
        wide[here, :] = source[here, :].astype(f32)
        return carry

    lax.fori_loop(0, rows // 256, chunk, 0)


def pick_kernel(rows_ref, store_ref, out_ref, wide, picked):
    widen(store_ref, wide, STORE_ROWS)

    def one_peer(peer, carry):
        base = pl.multiple_of(peer * CAP, CAP)
        for slot in range(CAP):
            picked[pl.ds(base + slot, 1), :] = wide[pl.ds(rows_ref[peer, slot], 1), :]
        out_ref[pl.ds(base, CAP), :] = picked[pl.ds(base, CAP), :].astype(bf16)
        return carry

    lax.fori_loop(0, PEERS, one_peer, 0)


def pick_rows(send_rows, store):
    return pl.pallas_call(
        pick_kernel,
        name="pick_rows",
        out_shape=shape((TABLE, F), bf16),
        in_specs=[SMEM, VMEM],
        out_specs=VMEM,
        scratch_shapes=[pltpu.VMEM((STORE_ROWS, F), f32), pltpu.VMEM((TABLE, F), f32)],
        compiler_params=LIMIT,
        cost_estimate=pl.CostEstimate(flops=0, bytes_accessed=2 << 20, transcendentals=0),
    )(send_rows, store)


def as_column(row):
    return jnp.broadcast_to(row.astype(f32), (128, 128)).T


def slot_counts(table):
    places = lax.broadcasted_iota(jnp.int32, (M1, M2), 0)
    degree = table[11:12, :]
    counts = jnp.zeros((M1, M2), f32)
    for k in range(FAN2):
        live = (places == table[k : k + 1, :]) & (degree > k)
        counts = counts + live.astype(f32)
    chosen = (places == table[10:11, :]).astype(f32)
    return chosen.astype(bf16), counts.astype(bf16)


def over_rows(a, b):
    return lax.dot_general(a, b, (((0,), (0,)), ((), ())), preferred_element_type=f32)


def elu(v):
    return jnp.where(v > 0, v, jnp.exp(jnp.minimum(v, 0.0)) - 1.0)


def slope(v):
    return jnp.where(v > 0, 1.0, jnp.exp(jnp.minimum(v, 0.0)))


def forward_kernel(
    core_ref, targets_ref, neighbors_ref, degree_ref, table_ref, arrived_ref, w1_ref, w2_ref, cot_ref,
    joined_ref, pre_ref, hidden_two_ref, grad_two_ref, keep_ref, send_ref,
    wide, chosen, summed, hidden,
):
    widen(arrived_ref, wide, TABLE)
    wide[TABLE : TABLE + 8, :] = jnp.zeros((8, F), f32)

    def eight_nodes(step, carry):
        base = pl.multiple_of(step * 8, 8)
        for lane in range(8):
            node = base + lane
            chosen[pl.ds(node, 1), :] = wide[pl.ds(targets_ref[node], 1), :]
            terms = [wide[pl.ds(neighbors_ref[k, node], 1), :] for k in range(FAN1)]
            while len(terms) > 1:
                pairs = [a + b for a, b in zip(terms[::2], terms[1::2])]
                terms = pairs + ([terms[-1]] if len(terms) % 2 else [])
            summed[pl.ds(node, 1), :] = terms[0]
        return carry

    lax.fori_loop(0, M1 // 8, eight_nodes, 0)

    for block in range(M1 // 128):
        rows = slice(block * 128, block * 128 + 128)
        degree = as_column(degree_ref[block : block + 1, :])
        joined_ref[rows, :F] = chosen[rows, :].astype(bf16)
        joined_ref[rows, F:] = (summed[rows, :] / degree).astype(bf16)
        pre = jnp.dot(joined_ref[rows, :], w1_ref[...], preferred_element_type=f32)
        pre_ref[rows, :] = pre
        hidden[rows, :] = elu(pre).astype(bf16)

    table = table_ref[...]
    onehot, counts = slot_counts(table)
    own = over_rows(onehot, hidden[...]).astype(bf16)
    degree = as_column(table[11:12, :])
    mean = (over_rows(counts, hidden[...]) / jnp.tile(degree, (1, H // 128))).astype(bf16)
    pre_two = jnp.dot(own, w2_ref[:H, :], preferred_element_type=f32) + jnp.dot(
        mean, w2_ref[H:, :], preferred_element_type=f32
    )
    hidden_two_ref[...] = elu(pre_two).astype(bf16)
    grad_two_ref[...] = (cot_ref[...].astype(f32) * slope(pre_two)).astype(bf16)
    first = core_ref[0] == 0

    @pl.when(first)
    def _():
        keep_ref[...] = own
        send_ref[...] = mean

    @pl.when(jnp.logical_not(first))
    def _():
        keep_ref[...] = mean
        send_ref[...] = own


def forward(core, targets, neighbors, degree, table, arrived, w1, w2, cot):
    return pl.pallas_call(
        forward_kernel,
        name="forward",
        out_shape=(
            shape((M1, 2 * F), bf16),
            shape((M1, H), f32),
            shape((M2, H), bf16),
            shape((M2, H), bf16),
            shape((M2, H), bf16),
            shape((M2, H), bf16),
        ),
        in_specs=[SMEM, SMEM, SMEM] + [VMEM] * 6,
        out_specs=[VMEM] * 6,
        scratch_shapes=[
            pltpu.VMEM((TABLE + 8, F), f32),
            pltpu.VMEM((M1, F), f32),
            pltpu.VMEM((M1, F), f32),
            pltpu.VMEM((M1, H), bf16),
        ],
        compiler_params=LIMIT,
        cost_estimate=pl.CostEstimate(flops=1 << 30, bytes_accessed=10 << 20, transcendentals=1 << 19),
    )(core, targets, neighbors, degree, table, arrived, w1, w2, cot)


def backward_kernel(table_ref, grad_two_ref, w2_ref, pre_ref, joined_ref, out_ref, stacked, spread, grad_pre):
    table = table_ref[...]
    grad_two = grad_two_ref[...]
    onehot, counts = slot_counts(table)
    stacked[:, :128] = onehot
    stacked[:, 128:256] = counts
    stacked[:, 256:] = counts
    dims = (((1,), (1,)), ((), ()))
    spread[:128, :] = lax.dot_general(grad_two, w2_ref[:H, :], dims, preferred_element_type=f32).astype(bf16)
    mean_grad = lax.dot_general(grad_two, w2_ref[H:, :], dims, preferred_element_type=f32).astype(bf16)
    degree = as_column(table[11:12, :])
    scaled = mean_grad.astype(f32) / jnp.tile(degree, (1, H // 128))
    high = scaled.astype(bf16)
    spread[128:256, :] = high
    spread[256:, :] = (scaled - high.astype(f32)).astype(bf16)
    for block in range(M1 // 128):
        rows = slice(block * 128, block * 128 + 128)
        grad_hidden = jnp.dot(stacked[rows, :], spread[...], preferred_element_type=f32).astype(bf16)
        grad_pre[rows, :] = (grad_hidden.astype(f32) * slope(pre_ref[rows, :])).astype(bf16)
    grad_one = over_rows(grad_pre[...], joined_ref[...]).astype(bf16)
    for xh in range(2):
        for rest in range(8):
            out_ref[xh * 8 + rest] = grad_one[rest * 128 : rest * 128 + 128, xh * 128 : xh * 128 + 128]


def backward(table, grad_two, w2, pre, joined):
    return pl.pallas_call(
        backward_kernel,
        name="backward",
        out_shape=shape((16, 128, 128), bf16),
        in_specs=[VMEM] * 5,
        out_specs=VMEM,
        scratch_shapes=[
            pltpu.VMEM((M1, 384), bf16),
            pltpu.VMEM((384, H), bf16),
            pltpu.VMEM((M1, H), bf16),
        ],
        compiler_params=LIMIT,
        cost_estimate=pl.CostEstimate(flops=1 << 30, bytes_accessed=8 << 20, transcendentals=1 << 19),
    )(table, grad_two, w2, pre, joined)


def product_kernel(mine_ref, theirs_ref, keep_ref, got_ref, one_ref, out_ref):
    for rest in range(8):
        rows = slice(rest * 128, rest * 128 + 128)
        product = over_rows(mine_ref[:, rows], keep_ref[...]) + over_rows(theirs_ref[:, rows], got_ref[...])
        product = product.astype(bf16)
        for xh in range(2):
            for block in range(4):
                column = (xh * 4 + block) * 128
                out_ref[xh * 8 + rest, block] = product[:, column : column + 128]
            out_ref[xh * 8 + rest, 4] = one_ref[xh * 8 + rest]


def product(mine, theirs, keep, got, one):
    return pl.pallas_call(
        product_kernel,
        name="product",
        out_shape=shape((16, 5, 128, 128), bf16),
        in_specs=[VMEM] * 5,
        out_specs=VMEM,
        compiler_params=LIMIT,
        cost_estimate=pl.CostEstimate(flops=1 << 29, bytes_accessed=4 << 20, transcendentals=0),
    )(mine, theirs, keep, got, one)


def turned(value, axes, count, steps):
    pairs = [(source, (source + steps) % count) for source in range(count)]
    return lax.ppermute(value, axes, pairs)


def per_device(
    feature_store, send_rows, send_counts, target_one, neighbor_one, degree_one,
    target_two, neighbor_two, degree_two, weight_one, weight_two, cotangent,
):
    core = lax.axis_index("core")
    table = jnp.concatenate([neighbor_two, target_two[None], degree_two[None], jnp.zeros((4, M2), jnp.int32)], axis=0)
    table = turned(table, SEC, 4, -1)
    cot = turned(cotangent, SEC, 4, -1)

    outgoing = pick_rows(send_rows, feature_store).reshape(PEERS, CAP, F)
    arrived = lax.all_to_all(outgoing, DEV, split_axis=0, concat_axis=0, tiled=True).reshape(TABLE, F)

    live = lax.broadcasted_iota(jnp.int32, (FAN1, M1), 0) < degree_one[None, :]
    neighbors = jnp.where(live, neighbor_one, TABLE)
    joined, pre, hidden_two, grad_two, keep, send = forward(
        core.reshape(1).astype(jnp.int32), target_one, neighbors, degree_one.reshape(4, 128), table, arrived,
        weight_one, weight_two, cot,
    )
    theirs = turned(grad_two, "core", 2, 1)
    got = turned(send, "core", 2, 1)
    hidden_two = turned(hidden_two, SEC, 4, 1)
    one = backward(table, grad_two, weight_two, pre, joined)
    parts = product(grad_two, theirs, keep, got, one)

    parts = lax.all_to_all(parts, PLANE, split_axis=0, concat_axis=0, tiled=True)
    summed = jnp.sum(parts.astype(f32), axis=0).astype(bf16)
    summed = summed.reshape(5, 8, 16, 128).transpose(1, 0, 2, 3)
    summed = lax.all_to_all(summed, "z", split_axis=0, concat_axis=0, tiled=True)
    mine = jnp.sum(summed.astype(f32), axis=0)
    pieces = [mine] + [turned(mine, SEC, 4, k) for k in (1, 2, 3)]
    place = lax.axis_index(SEC)
    ordered = jnp.zeros((4, 5, 16, 128), f32)
    for k, piece in enumerate(pieces):
        ordered = lax.dynamic_update_slice(ordered, piece[None], ((place - k) % 4, 0, 0, 0))
    by_place = ordered.reshape(2, 2, 5, 16, 128)
    grad_two_out = by_place[:, :, :4].transpose(3, 1, 0, 2, 4).reshape(16, 2 * H)
    grad_one_out = by_place[:, :, 4].sum(axis=1).transpose(1, 0, 2).reshape(16, 2 * F)
    return hidden_two, grad_one_out, grad_two_out


def solution(mesh):
    fine = Mesh(mesh.devices.reshape(2, 2, 2, 4, 8), AXES)
    both = SEC + DEV
    return jax.shard_map(
        per_device,
        mesh=fine,
        in_specs=(
            P(both, None), P(both, None), P(both), P(both), P(None, both), P(both),
            P(both), P(None, both), P(both), P(), P(), P(both, None),
        ),
        out_specs=(P(both, None), P(DEV, None), P(DEV, None)),
        check_vma=False,
    )
```

```python
import functools

import jax
import jax.numpy as jnp
from jax import lax
from jax.experimental import pallas as pl
from jax.experimental.pallas import tpu as pltpu
from jax.sharding import PartitionSpec as P


F = 128
H = 1024
FAN1 = 15
FAN2 = 10
CAP = 64
STORE_ROWS = 4096
M2 = 128
M1 = 512
PEERS = 64
TABLE = PEERS * CAP
DEVICES = 256
ALL = ("sec", "dev")

bf16 = jnp.bfloat16
f32 = jnp.float32
VMEM = pl.BlockSpec(memory_space=pltpu.VMEM)
SMEM = pl.BlockSpec(memory_space=pltpu.SMEM)
HBM = pl.BlockSpec(memory_space=pltpu.HBM)


def limit(mib):
    return pltpu.CompilerParams(vmem_limit_bytes=mib * 1024 * 1024)


def shape(dims, dtype):
    return jax.ShapeDtypeStruct(dims, dtype)


def widen(source, wide, rows):
    def chunk(step, carry):
        here = pl.ds(pl.multiple_of(step * 256, 256), 256)
        wide[here, :] = source[here, :].astype(f32)
        return carry

    lax.fori_loop(0, rows // 256, chunk, 0)


def pick_kernel(rows_ref, store_ref, out_ref, wide, picked):
    widen(store_ref, wide, STORE_ROWS)

    for peer in range(PEERS):
        base = peer * CAP
        for slot in range(CAP):
            picked[base + slot : base + slot + 1, :] = wide[pl.ds(rows_ref[peer, slot], 1), :]
        out_ref[base : base + CAP, :] = picked[base : base + CAP, :].astype(bf16)


def pick_rows(send_rows, store):
    return pl.pallas_call(
        pick_kernel,
        name="pick_rows",
        out_shape=shape((TABLE, F), bf16),
        in_specs=[SMEM, VMEM],
        out_specs=VMEM,
        scratch_shapes=[pltpu.VMEM((STORE_ROWS, F), f32), pltpu.VMEM((TABLE, F), f32)],
        compiler_params=limit(10),
        cost_estimate=pl.CostEstimate(flops=0, bytes_accessed=2 << 20, transcendentals=0),
    )(send_rows, store)


def as_column(row):
    return jnp.broadcast_to(row.astype(f32), (128, 128)).T


def slot_counts(table):
    places = lax.broadcasted_iota(jnp.int32, (M1, M2), 0)
    degree = table[11:12, :]
    counts = jnp.zeros((M1, M2), f32)
    for k in range(FAN2):
        live = (places == table[k : k + 1, :]) & (degree > k)
        counts = counts + live.astype(f32)
    chosen = (places == table[10:11, :]).astype(f32)
    return chosen.astype(bf16), counts.astype(bf16)


def over_rows(a, b):
    return lax.dot_general(a, b, (((0,), (0,)), ((), ())), preferred_element_type=f32)


def elu(v):
    return jnp.where(v > 0, v, jnp.exp(jnp.minimum(v, 0.0)) - 1.0)


def slope(v):
    return jnp.where(v > 0, 1.0, jnp.exp(jnp.minimum(v, 0.0)))


def forward_kernel(
    core_ref, slots_ref, degree_ref, table_ref, arrived_ref, w1_ref, cot_ref, w2_hbm,
    joined_ref, pre_ref, hidden_two_ref, grad_two_ref, keep_ref, send_ref,
    wide, chosen, summed, hidden, w2_ref, w2_sem,
):
    load = pltpu.make_async_copy(w2_hbm, w2_ref, w2_sem)
    load.start()
    widen(arrived_ref, wide, TABLE)
    wide[TABLE : TABLE + 8, :] = jnp.zeros((8, F), f32)

    for node in range(M1):
        wanted = [slots_ref[node // 8, node % 8 * 16 + k] for k in range(16)]
        chosen[node : node + 1, :] = wide[pl.ds(wanted[15], 1), :]
        terms = [wide[pl.ds(wanted[k], 1), :] for k in range(FAN1)]
        while len(terms) > 1:
            pairs = [a + b for a, b in zip(terms[::2], terms[1::2])]
            terms = pairs + ([terms[-1]] if len(terms) % 2 else [])
        summed[node : node + 1, :] = terms[0]

    for block in range(M1 // 128):
        rows = slice(block * 128, block * 128 + 128)
        degree = as_column(degree_ref[block : block + 1, :])
        joined_ref[rows, :F] = chosen[rows, :].astype(bf16)
        joined_ref[rows, F:] = (summed[rows, :] / degree).astype(bf16)
        pre = jnp.dot(joined_ref[rows, :], w1_ref[...], preferred_element_type=f32)
        pre_ref[rows, :] = pre
        hidden[rows, :] = elu(pre).astype(bf16)

    table = table_ref[...]
    onehot, counts = slot_counts(table)
    own = over_rows(onehot, hidden[...]).astype(bf16)
    degree = as_column(table[11:12, :])
    mean = (over_rows(counts, hidden[...]) / jnp.tile(degree, (1, H // 128))).astype(bf16)
    load.wait()
    pre_two = jnp.dot(own, w2_ref[:H, :], preferred_element_type=f32) + jnp.dot(
        mean, w2_ref[H:, :], preferred_element_type=f32
    )
    hidden_two_ref[...] = elu(pre_two).astype(bf16)
    grad_two_ref[...] = (cot_ref[...].astype(f32) * slope(pre_two)).astype(bf16)
    first = core_ref[0] == 0

    @pl.when(first)
    def _():
        keep_ref[...] = own
        send_ref[...] = mean

    @pl.when(jnp.logical_not(first))
    def _():
        keep_ref[...] = mean
        send_ref[...] = own


def forward(core, slots, degree, table, arrived, w1, cot, w2):
    return pl.pallas_call(
        forward_kernel,
        name="forward",
        out_shape=(
            shape((M1, 2 * F), bf16),
            shape((M1, H), f32),
            shape((M2, H), bf16),
            shape((M2, H), bf16),
            shape((M2, H), bf16),
            shape((M2, H), bf16),
        ),
        in_specs=[SMEM, SMEM] + [VMEM] * 5 + [HBM],
        out_specs=[VMEM] * 6,
        scratch_shapes=[
            pltpu.VMEM((TABLE + 8, F), f32),
            pltpu.VMEM((M1, F), f32),
            pltpu.VMEM((M1, F), f32),
            pltpu.VMEM((M1, H), bf16),
            pltpu.VMEM((2 * H, H), bf16),
            pltpu.SemaphoreType.DMA,
        ],
        compiler_params=limit(20),
        cost_estimate=pl.CostEstimate(flops=1 << 30, bytes_accessed=10 << 20, transcendentals=1 << 19),
    )(core, slots, degree, table, arrived, w1, cot, w2)


def backward_kernel(table_ref, grad_two_ref, w2_ref, pre_ref, joined_ref, out_ref, stacked, spread, grad_pre):
    table = table_ref[...]
    grad_two = grad_two_ref[...]
    onehot, counts = slot_counts(table)
    stacked[:, :128] = onehot
    stacked[:, 128:256] = counts
    stacked[:, 256:] = counts
    dims = (((1,), (1,)), ((), ()))
    spread[:128, :] = lax.dot_general(grad_two, w2_ref[:H, :], dims, preferred_element_type=f32).astype(bf16)
    mean_grad = lax.dot_general(grad_two, w2_ref[H:, :], dims, preferred_element_type=f32).astype(bf16)
    degree = as_column(table[11:12, :])
    scaled = mean_grad.astype(f32) / jnp.tile(degree, (1, H // 128))
    high = scaled.astype(bf16)
    spread[128:256, :] = high
    spread[256:, :] = (scaled - high.astype(f32)).astype(bf16)
    for block in range(M1 // 128):
        rows = slice(block * 128, block * 128 + 128)
        grad_hidden = jnp.dot(stacked[rows, :], spread[...], preferred_element_type=f32).astype(bf16)
        grad_pre[rows, :] = (grad_hidden.astype(f32) * slope(pre_ref[rows, :])).astype(bf16)
    grad_one = over_rows(grad_pre[...], joined_ref[...]).astype(bf16)
    for xh in range(2):
        for rest in range(8):
            out_ref[xh * 8 + rest] = grad_one[rest * 128 : rest * 128 + 128, xh * 128 : xh * 128 + 128]


def backward(table, grad_two, w2, pre, joined):
    return pl.pallas_call(
        backward_kernel,
        name="backward",
        out_shape=shape((16, 128, 128), bf16),
        in_specs=[VMEM] * 5,
        out_specs=VMEM,
        scratch_shapes=[
            pltpu.VMEM((M1, 384), bf16),
            pltpu.VMEM((384, H), bf16),
            pltpu.VMEM((M1, H), bf16),
        ],
        compiler_params=limit(20),
        cost_estimate=pl.CostEstimate(flops=1 << 30, bytes_accessed=8 << 20, transcendentals=1 << 19),
    )(table, grad_two, w2, pre, joined)


def product_kernel(core_ref, mine_ref, theirs_ref, keep_ref, got_ref, one_ref, out_ref):
    first = core_ref[0] == 0
    for rest in range(8):
        rows = slice(rest * 128, rest * 128 + 128)
        product = over_rows(mine_ref[:, rows], keep_ref[...]) + over_rows(theirs_ref[:, rows], got_ref[...])
        product = product.astype(bf16)
        for xh in range(2):
            along_x, along_y = xh * 2 + rest // 4, rest % 4
            place = jnp.where(first, along_x * 4 + along_y, along_y * 4 + along_x)
            for block in range(4):
                column = (xh * 4 + block) * 128
                out_ref[place, block] = product[:, column : column + 128]
            out_ref[place, 4] = one_ref[xh * 8 + rest]


def product(core, mine, theirs, keep, got, one):
    return pl.pallas_call(
        product_kernel,
        name="product",
        out_shape=shape((16, 5, 128, 128), bf16),
        in_specs=[SMEM] + [VMEM] * 5,
        out_specs=VMEM,
        compiler_params=limit(10),
        cost_estimate=pl.CostEstimate(flops=1 << 29, bytes_accessed=4 << 20, transcendentals=0),
    )(core, mine, theirs, keep, got, one)


def flat(xh, core, xl, y, z):
    return ((((xh * 2 + core) * 2 + xl) * 4 + y) * 8) + z


def parts_of(device):
    return device // 128, device // 64 % 2, device // 32 % 2, device // 8 % 4, device % 8


def in_section(device, steps):
    return (device + steps * PEERS) % DEVICES


def other_core(device):
    return device ^ 64


def permuted(value, target):
    return lax.ppermute(value, ALL, [(device, target(device)) for device in range(DEVICES)])


DEV_GROUPS = [[section * PEERS + peer for peer in range(PEERS)] for section in range(4)]
Z_GROUPS = [[row * 8 + z for z in range(8)] for row in range(DEVICES // 8)]


def x_line(core, y, z):
    return [flat(xh, core, xl, y, z) for xh in range(2) for xl in range(2)]


def y_line(xh, core, xl, z):
    return [flat(xh, core, xl, y, z) for y in range(4)]


def lines(x_core):
    along_x = [x_line(x_core, y, z) for y in range(4) for z in range(8)]
    along_y = [y_line(xh, 1 - x_core, xl, z) for xh in range(2) for xl in range(2) for z in range(8)]
    return along_x + along_y


def exchanged(value, groups):
    return lax.all_to_all(value, ALL, 0, 0, axis_index_groups=groups, tiled=True)


def per_device(
    feature_store, send_rows, send_counts, target_one, neighbor_one, degree_one,
    target_two, neighbor_two, degree_two, weight_one, weight_two, cotangent,
):
    me = lax.axis_index(ALL).astype(jnp.int32)
    core = (me // 64 % 2).reshape(1)
    table = jnp.concatenate([neighbor_two, target_two[None], degree_two[None], jnp.zeros((4, M2), jnp.int32)], axis=0)
    table = permuted(table, lambda device: in_section(device, -1))
    cot = permuted(cotangent, lambda device: in_section(device, -1))

    outgoing = pick_rows(send_rows, feature_store).reshape(PEERS, CAP, F)
    arrived = exchanged(outgoing, DEV_GROUPS).reshape(TABLE, F)

    live = lax.broadcasted_iota(jnp.int32, (FAN1, M1), 0) < degree_one[None, :]
    slots = jnp.concatenate([jnp.where(live, neighbor_one, TABLE), target_one[None]], axis=0)
    slots = slots.T.reshape(M1 // 8, 128)
    joined, pre, hidden_two, grad_two, keep, send = forward(
        core, slots, degree_one.reshape(4, 128), table, arrived, weight_one, cot,
        pltpu.with_memory_space_constraint(weight_two, pltpu.HBM),
    )
    theirs = permuted(grad_two, other_core)
    got = permuted(send, other_core)
    hidden_two = permuted(hidden_two, lambda device: in_section(device, 1))
    one = backward(table, grad_two, weight_two, pre, joined)
    parts = product(core, grad_two, theirs, keep, got, one)

    parts = exchanged(parts, lines(0)).reshape(4, 4, 5, 128, 128)
    parts = exchanged(jnp.sum(parts.astype(f32), axis=0).astype(bf16), lines(1))
    summed = jnp.sum(parts.astype(f32), axis=0).astype(bf16)
    summed = summed.reshape(5, 8, 16, 128).transpose(1, 0, 2, 3)
    summed = exchanged(summed, Z_GROUPS)
    mine = jnp.sum(summed.astype(f32), axis=0)
    pieces = [mine] + [permuted(mine, functools.partial(in_section, steps=k)) for k in (1, 2, 3)]
    place = me // PEERS
    ordered = jnp.zeros((4, 5, 16, 128), f32)
    for k, piece in enumerate(pieces):
        ordered = lax.dynamic_update_slice(ordered, piece[None], ((place - k) % 4, 0, 0, 0))
    by_place = ordered.reshape(2, 2, 5, 16, 128)
    grad_two_out = by_place[:, :, :4].transpose(3, 1, 0, 2, 4).reshape(16, 2 * H)
    grad_one_out = by_place[:, :, 4].sum(axis=1).transpose(1, 0, 2).reshape(16, 2 * F)
    return hidden_two, grad_one_out, grad_two_out


def solution(mesh):
    return jax.shard_map(
        per_device,
        mesh=mesh,
        in_specs=(
            P(ALL, None), P(ALL, None), P(ALL), P(ALL), P(None, ALL), P(ALL),
            P(ALL), P(None, ALL), P(ALL), P(), P(), P(ALL, None),
        ),
        out_specs=(P(ALL, None), P("dev", None), P("dev", None)),
        check_vma=False,
    )
```

```python
import jax
import jax.numpy as jnp
from jax import lax
from jax.experimental import pallas as pl
from jax.experimental.pallas import tpu as pltpu
from jax.sharding import PartitionSpec as P


F = 128
H = 1024
FAN1 = 15
FAN2 = 10
CAP = 64
STORE_ROWS = 4096
M2 = 128
M1 = 512
PEERS = 64
TABLE = PEERS * CAP
DEVICES = 256
ALL = ("sec", "dev")

bf16 = jnp.bfloat16
f32 = jnp.float32
VMEM = pl.BlockSpec(memory_space=pltpu.VMEM)
SMEM = pl.BlockSpec(memory_space=pltpu.SMEM)
HBM = pl.BlockSpec(memory_space=pltpu.HBM)


def limit(mib):
    return pltpu.CompilerParams(vmem_limit_bytes=mib * 1024 * 1024)


def shape(dims, dtype):
    return jax.ShapeDtypeStruct(dims, dtype)


def widen(source, wide, rows):
    def chunk(step, carry):
        here = pl.ds(pl.multiple_of(step * 256, 256), 256)
        wide[here, :] = source[here, :].astype(f32)
        return carry

    lax.fori_loop(0, rows // 256, chunk, 0)


def pick_kernel(rows_ref, store_ref, out_ref, wide, picked):
    widen(store_ref, wide, STORE_ROWS)

    for peer in range(PEERS):
        base = peer * CAP
        for slot in range(CAP):
            picked[base + slot : base + slot + 1, :] = wide[pl.ds(rows_ref[peer, slot], 1), :]
        out_ref[base : base + CAP, :] = picked[base : base + CAP, :].astype(bf16)


def pick_rows(send_rows, store):
    return pl.pallas_call(
        pick_kernel,
        name="pick_rows",
        out_shape=shape((TABLE, F), bf16),
        in_specs=[SMEM, VMEM],
        out_specs=VMEM,
        scratch_shapes=[pltpu.VMEM((STORE_ROWS, F), f32), pltpu.VMEM((TABLE, F), f32)],
        compiler_params=limit(10),
        cost_estimate=pl.CostEstimate(flops=0, bytes_accessed=2 << 20, transcendentals=0),
    )(send_rows, store)


def tables_kernel(n1_ref, d1_ref, t1_ref, n2_ref, d2_ref, t2_ref, slots_ref, table_ref):
    order = lax.broadcasted_iota(jnp.int32, (FAN1, M1), 0)
    slots_ref[:FAN1, :] = jnp.where(order < d1_ref[...], n1_ref[...], TABLE)
    slots_ref[FAN1:, :] = t1_ref[...]
    table_ref[:FAN2, :] = n2_ref[...]
    table_ref[FAN2 : FAN2 + 1, :] = t2_ref[...]
    table_ref[FAN2 + 1 : FAN2 + 2, :] = d2_ref[...]
    table_ref[FAN2 + 2 :, :] = jnp.zeros((14 - FAN2, M2), jnp.int32)


def tables(n1, d1, t1, n2, d2, t2):
    return pl.pallas_call(
        tables_kernel,
        name="tables",
        out_shape=(shape((FAN1 + 1, M1), jnp.int32), shape((16, M2), jnp.int32)),
        in_specs=[VMEM] * 6,
        out_specs=[VMEM] * 2,
        compiler_params=limit(2),
    )(n1, d1.reshape(1, M1), t1.reshape(1, M1), n2, d2.reshape(1, M2), t2.reshape(1, M2))


def as_column(row):
    return jnp.broadcast_to(row.astype(f32), (128, 128)).T


def slot_counts(table):
    places = lax.broadcasted_iota(jnp.int32, (M1, M2), 0)
    degree = table[11:12, :]
    counts = jnp.zeros((M1, M2), f32)
    for k in range(FAN2):
        live = (places == table[k : k + 1, :]) & (degree > k)
        counts = counts + live.astype(f32)
    chosen = (places == table[10:11, :]).astype(f32)
    return chosen.astype(bf16), counts.astype(bf16)


def over_rows(a, b):
    return lax.dot_general(a, b, (((0,), (0,)), ((), ())), preferred_element_type=f32)


def elu(v):
    return jnp.where(v > 0, v, jnp.exp(jnp.minimum(v, 0.0)) - 1.0)


def slope(v):
    return jnp.where(v > 0, 1.0, jnp.exp(jnp.minimum(v, 0.0)))


def forward_kernel(
    me_ref, slots_ref, degree_ref, table_ref, arrived_ref, cot_ref, w1_hbm, w2_hbm,
    joined_ref, pre_ref, hidden_two_ref, grad_two_ref, keep_ref, send_ref,
    wide, chosen, summed, hidden, w1_ref, w2_ref, w1_sem, w2_sem,
):
    load_one = pltpu.make_async_copy(w1_hbm, w1_ref, w1_sem)
    load_two = pltpu.make_async_copy(w2_hbm, w2_ref, w2_sem)
    load_one.start()
    load_two.start()
    widen(arrived_ref, wide, TABLE)
    wide[TABLE : TABLE + 8, :] = jnp.zeros((8, F), f32)

    for node in range(M1):
        wanted = [slots_ref[k, node] for k in range(16)]
        chosen[node : node + 1, :] = wide[pl.ds(wanted[15], 1), :]
        terms = [wide[pl.ds(wanted[k], 1), :] for k in range(FAN1)]
        while len(terms) > 1:
            pairs = [a + b for a, b in zip(terms[::2], terms[1::2])]
            terms = pairs + ([terms[-1]] if len(terms) % 2 else [])
        summed[node : node + 1, :] = terms[0]

    load_one.wait()
    for block in range(M1 // 128):
        rows = slice(block * 128, block * 128 + 128)
        degree = as_column(degree_ref[block : block + 1, :])
        joined_ref[rows, :F] = chosen[rows, :].astype(bf16)
        joined_ref[rows, F:] = (summed[rows, :] / degree).astype(bf16)
        pre = jnp.dot(joined_ref[rows, :], w1_ref[...], preferred_element_type=f32)
        pre_ref[rows, :] = pre
        hidden[rows, :] = elu(pre).astype(bf16)

    table = table_ref[...]
    onehot, counts = slot_counts(table)
    own = over_rows(onehot, hidden[...]).astype(bf16)
    degree = as_column(table[11:12, :])
    mean = (over_rows(counts, hidden[...]) / jnp.tile(degree, (1, H // 128))).astype(bf16)
    load_two.wait()
    pre_two = jnp.dot(own, w2_ref[:H, :], preferred_element_type=f32) + jnp.dot(
        mean, w2_ref[H:, :], preferred_element_type=f32
    )
    hidden_two_ref[...] = elu(pre_two).astype(bf16)
    grad_two_ref[...] = (cot_ref[...].astype(f32) * slope(pre_two)).astype(bf16)
    first = me_ref[0] // PEERS % 2 == 0

    @pl.when(first)
    def _():
        keep_ref[...] = own
        send_ref[...] = mean

    @pl.when(jnp.logical_not(first))
    def _():
        keep_ref[...] = mean
        send_ref[...] = own


def forward(me, slots, degree, table, arrived, cot, w1, w2):
    return pl.pallas_call(
        forward_kernel,
        name="forward",
        out_shape=(
            shape((M1, 2 * F), bf16),
            shape((M1, H), f32),
            shape((M2, H), bf16),
            shape((M2, H), bf16),
            shape((M2, H), bf16),
            shape((M2, H), bf16),
        ),
        in_specs=[SMEM, SMEM] + [VMEM] * 4 + [HBM, HBM],
        out_specs=[VMEM] * 6,
        scratch_shapes=[
            pltpu.VMEM((TABLE + 8, F), f32),
            pltpu.VMEM((M1, F), f32),
            pltpu.VMEM((M1, F), f32),
            pltpu.VMEM((M1, H), bf16),
            pltpu.VMEM((2 * F, H), bf16),
            pltpu.VMEM((2 * H, H), bf16),
            pltpu.SemaphoreType.DMA,
            pltpu.SemaphoreType.DMA,
        ],
        compiler_params=limit(20),
        cost_estimate=pl.CostEstimate(flops=1 << 30, bytes_accessed=10 << 20, transcendentals=1 << 19),
    )(me, slots, degree, table, arrived, cot, w1, w2)


def backward_kernel(table_ref, grad_two_ref, w2_ref, pre_ref, joined_ref, out_ref, stacked, spread, grad_pre):
    table = table_ref[...]
    grad_two = grad_two_ref[...]
    onehot, counts = slot_counts(table)
    stacked[:, :128] = onehot
    stacked[:, 128:256] = counts
    stacked[:, 256:] = counts
    dims = (((1,), (1,)), ((), ()))
    spread[:128, :] = lax.dot_general(grad_two, w2_ref[:H, :], dims, preferred_element_type=f32).astype(bf16)
    mean_grad = lax.dot_general(grad_two, w2_ref[H:, :], dims, preferred_element_type=f32).astype(bf16)
    degree = as_column(table[11:12, :])
    scaled = mean_grad.astype(f32) / jnp.tile(degree, (1, H // 128))
    high = scaled.astype(bf16)
    spread[128:256, :] = high
    spread[256:, :] = (scaled - high.astype(f32)).astype(bf16)
    for block in range(M1 // 128):
        rows = slice(block * 128, block * 128 + 128)
        grad_hidden = jnp.dot(stacked[rows, :], spread[...], preferred_element_type=f32).astype(bf16)
        grad_pre[rows, :] = (grad_hidden.astype(f32) * slope(pre_ref[rows, :])).astype(bf16)
    grad_one = over_rows(grad_pre[...], joined_ref[...]).astype(bf16)
    for xh in range(2):
        for rest in range(8):
            out_ref[xh * 8 + rest] = grad_one[rest * 128 : rest * 128 + 128, xh * 128 : xh * 128 + 128]


def backward(table, grad_two, w2, pre, joined):
    return pl.pallas_call(
        backward_kernel,
        name="backward",
        out_shape=shape((16, 128, 128), bf16),
        in_specs=[VMEM] * 5,
        out_specs=VMEM,
        scratch_shapes=[
            pltpu.VMEM((M1, 384), bf16),
            pltpu.VMEM((384, H), bf16),
            pltpu.VMEM((M1, H), bf16),
        ],
        compiler_params=limit(20),
        cost_estimate=pl.CostEstimate(flops=1 << 30, bytes_accessed=8 << 20, transcendentals=1 << 19),
    )(table, grad_two, w2, pre, joined)


def place_of(me, xh, xl, y):
    swapped = me // PEERS % 2 == 0

    def split(target, half):
        near, far = (target // 2 + target % 2 + half) % 2, target // 2
        return jnp.where(swapped, near, far), jnp.where(swapped, far, target % 2)

    outer_x, inner_x = split(xh * 2 + xl, me // 128)
    outer_y, inner_y = split(y, me // 16 % 2)
    return ((outer_x * 2 + outer_y) * 2 + inner_x) * 2 + inner_y


def product_kernel(me_ref, mine_ref, theirs_ref, keep_ref, got_ref, one_ref, out_ref):
    for rest in range(8):
        rows = slice(rest * 128, rest * 128 + 128)
        product = over_rows(mine_ref[:, rows], keep_ref[...]) + over_rows(theirs_ref[:, rows], got_ref[...])
        product = product.astype(bf16)
        for xh in range(2):
            place = place_of(me_ref[0], xh, rest // 4, rest % 4)
            one = one_ref[xh * 8 + rest]
            for z in range(8):
                rows = slice(z * 16, z * 16 + 16)
                for block in range(4):
                    column = (xh * 4 + block) * 128
                    out_ref[place, z, block] = product[rows, column : column + 128]
                out_ref[place, z, 4] = one[rows, :]


def product(me, mine, theirs, keep, got, one):
    return pl.pallas_call(
        product_kernel,
        name="product",
        out_shape=shape((16, 8, 5, 16, 128), bf16),
        in_specs=[SMEM] + [VMEM] * 5,
        out_specs=VMEM,
        compiler_params=limit(10),
        cost_estimate=pl.CostEstimate(flops=1 << 29, bytes_accessed=4 << 20, transcendentals=0),
    )(me, mine, theirs, keep, got, one)


def sum_kernel(parts_ref, out_ref):
    total = parts_ref[0].astype(f32) + parts_ref[1].astype(f32)
    total = total + (parts_ref[2].astype(f32) + parts_ref[3].astype(f32))
    out_ref[...] = total.astype(bf16)


def sum_of_four(parts):
    return pl.pallas_call(
        sum_kernel,
        name="sum_of_four",
        out_shape=shape(parts.shape[1:], bf16),
        in_specs=[VMEM],
        out_specs=VMEM,
        compiler_params=limit(8),
    )(parts)


def spread_kernel(parts_ref, out_ref):
    total = parts_ref[0].astype(f32)
    for z in range(1, 8):
        total = total + parts_ref[z].astype(f32)
    for section in range(4):
        out_ref[section] = total


def spread_sum(parts):
    return pl.pallas_call(
        spread_kernel,
        name="spread_sum",
        out_shape=shape((4, 5, 16, 128), f32),
        in_specs=[VMEM],
        out_specs=VMEM,
        compiler_params=limit(4),
    )(parts)


def place_kernel(parts_ref, one_ref, two_ref):
    for xh in range(2):
        one_ref[:, xh * F : xh * F + F] = parts_ref[xh * 2, 4] + parts_ref[xh * 2 + 1, 4]
        for core in range(2):
            for block in range(4):
                column = core * H + xh * 512 + block * 128
                two_ref[:, column : column + 128] = parts_ref[xh * 2 + core, block]


def placed(parts):
    return pl.pallas_call(
        place_kernel,
        name="placed",
        out_shape=(shape((16, 2 * F), f32), shape((16, 2 * H), f32)),
        in_specs=[VMEM],
        out_specs=[VMEM] * 2,
        compiler_params=limit(4),
    )(parts)


def flat(xh, core, xl, y, z):
    return ((((xh * 2 + core) * 2 + xl) * 4 + y) * 8) + z


def in_section(device, steps):
    return (device + steps * PEERS) % DEVICES


def other_core(device):
    return device ^ 64


def permuted(value, target):
    return lax.ppermute(value, ALL, [(device, target(device)) for device in range(DEVICES)])


DEV_GROUPS = [[section * PEERS + peer for peer in range(PEERS)] for section in range(4)]
Z_GROUPS = [[row * 8 + z for z in range(8)] for row in range(DEVICES // 8)]


SEC_GROUPS = [[section * PEERS + peer for section in range(4)] for peer in range(PEERS)]
PAIRS = (((0, 1), (2, 3)), ((0, 3), (1, 2)))


def squares(first_core):
    groups = []
    for core in range(2):
        pairs = PAIRS[core ^ first_core]
        for z in range(8):
            for along_x in pairs:
                for along_y in pairs:
                    groups.append([flat(x // 2, core, x % 2, y, z) for x in along_x for y in along_y])
    return groups


def exchanged(value, groups):
    return lax.all_to_all(value, ALL, 0, 0, axis_index_groups=groups, tiled=True)


def per_device(
    feature_store, send_rows, send_counts, target_one, neighbor_one, degree_one,
    target_two, neighbor_two, degree_two, weight_one, weight_two, cotangent,
):
    me = lax.axis_index(ALL).astype(jnp.int32).reshape(1)
    slots, table = tables(neighbor_one, degree_one, target_one, neighbor_two, degree_two, target_two)
    table = permuted(table, lambda device: in_section(device, -1))
    cot = permuted(cotangent, lambda device: in_section(device, -1))

    outgoing = pick_rows(
        pltpu.with_memory_space_constraint(send_rows, pltpu.HBM),
        pltpu.with_memory_space_constraint(feature_store, pltpu.HBM),
    ).reshape(PEERS, CAP, F)
    arrived = exchanged(outgoing, DEV_GROUPS).reshape(TABLE, F)

    joined, pre, hidden_two, grad_two, keep, send = forward(
        me, slots, degree_one.reshape(4, 128), table, arrived, cot,
        pltpu.with_memory_space_constraint(weight_one, pltpu.HBM),
        pltpu.with_memory_space_constraint(weight_two, pltpu.HBM),
    )
    theirs = permuted(grad_two, other_core)
    got = permuted(send, other_core)
    hidden_two = permuted(hidden_two, lambda device: in_section(device, 1))
    one = backward(table, grad_two, weight_two, pre, joined)
    parts = product(me, grad_two, theirs, keep, got, one)

    parts = exchanged(parts, squares(0)).reshape(4, 4, 8, 5, 16, 128)
    parts = exchanged(sum_of_four(parts), squares(1))
    parts = exchanged(sum_of_four(parts), Z_GROUPS)
    grad_one_out, grad_two_out = placed(exchanged(spread_sum(parts), SEC_GROUPS))
    return hidden_two, grad_one_out, grad_two_out


def solution(mesh):
    return jax.shard_map(
        per_device,
        mesh=mesh,
        in_specs=(
            P(ALL, None), P(ALL, None), P(ALL), P(ALL), P(None, ALL), P(ALL),
            P(ALL), P(None, ALL), P(ALL), P(), P(), P(ALL, None),
        ),
        out_specs=(P(ALL, None), P("dev", None), P("dev", None)),
        check_vma=False,
    )
```

```python
import jax
import jax.numpy as jnp
from jax import lax
from jax.experimental import pallas as pl
from jax.experimental.pallas import tpu as pltpu
from jax.sharding import PartitionSpec as P


F = 128
H = 1024
FAN1 = 15
FAN2 = 10
CAP = 64
STORE_ROWS = 4096
M2 = 128
M1 = 512
PEERS = 64
TABLE = PEERS * CAP
DEVICES = 256
ALL = ("sec", "dev")

bf16 = jnp.bfloat16
f32 = jnp.float32
VMEM = pl.BlockSpec(memory_space=pltpu.VMEM)
SMEM = pl.BlockSpec(memory_space=pltpu.SMEM)
HBM = pl.BlockSpec(memory_space=pltpu.HBM)


def limit(mib):
    return pltpu.CompilerParams(vmem_limit_bytes=mib * 1024 * 1024)


def shape(dims, dtype):
    return jax.ShapeDtypeStruct(dims, dtype)


def widen(source, wide, rows):
    def chunk(step, carry):
        here = pl.ds(pl.multiple_of(step * 256, 256), 256)
        wide[here, :] = source[here, :].astype(f32)
        return carry

    lax.fori_loop(0, rows // 256, chunk, 0)


def pick_kernel(rows_ref, store_ref, out_ref, wide, picked):
    widen(store_ref, wide, STORE_ROWS)

    for peer in range(PEERS):
        base = peer * CAP
        for slot in range(CAP):
            picked[base + slot : base + slot + 1, :] = wide[pl.ds(rows_ref[peer, slot], 1), :]
        out_ref[base : base + CAP, :] = picked[base : base + CAP, :].astype(bf16)


def pick_rows(send_rows, store):
    return pl.pallas_call(
        pick_kernel,
        name="pick_rows",
        out_shape=shape((TABLE, F), bf16),
        in_specs=[SMEM, VMEM],
        out_specs=VMEM,
        scratch_shapes=[pltpu.VMEM((STORE_ROWS, F), f32), pltpu.VMEM((TABLE, F), f32)],
        compiler_params=limit(10),
        cost_estimate=pl.CostEstimate(flops=0, bytes_accessed=2 << 20, transcendentals=0),
    )(send_rows, store)


def tables_kernel(n1_ref, d1_ref, t1_ref, n2_ref, d2_ref, t2_ref, slots_ref, table_ref):
    order = lax.broadcasted_iota(jnp.int32, (FAN1, M1), 0)
    slots_ref[:FAN1, :] = jnp.where(order < d1_ref[...], n1_ref[...], TABLE)
    slots_ref[FAN1:, :] = t1_ref[...]
    table_ref[:FAN2, :] = n2_ref[...]
    table_ref[FAN2 : FAN2 + 1, :] = t2_ref[...]
    table_ref[FAN2 + 1 : FAN2 + 2, :] = d2_ref[...]
    table_ref[FAN2 + 2 :, :] = jnp.zeros((14 - FAN2, M2), jnp.int32)


def tables(n1, d1, t1, n2, d2, t2):
    return pl.pallas_call(
        tables_kernel,
        name="tables",
        out_shape=(shape((FAN1 + 1, M1), jnp.int32), shape((16, M2), jnp.int32)),
        in_specs=[VMEM] * 6,
        out_specs=[VMEM] * 2,
        compiler_params=limit(2),
    )(n1, d1.reshape(1, M1), t1.reshape(1, M1), n2, d2.reshape(1, M2), t2.reshape(1, M2))


def as_column(row):
    return jnp.broadcast_to(row.astype(f32), (128, 128)).T


def slot_counts(table):
    places = lax.broadcasted_iota(jnp.int32, (M1, M2), 0)
    degree = table[11:12, :]
    counts = jnp.zeros((M1, M2), f32)
    for k in range(FAN2):
        live = (places == table[k : k + 1, :]) & (degree > k)
        counts = counts + live.astype(f32)
    chosen = (places == table[10:11, :]).astype(f32)
    return chosen.astype(bf16), counts.astype(bf16)


def over_rows(a, b):
    return lax.dot_general(a, b, (((0,), (0,)), ((), ())), preferred_element_type=f32)


def elu(v):
    return jnp.where(v > 0, v, jnp.exp(jnp.minimum(v, 0.0)) - 1.0)


def slope(v):
    return jnp.where(v > 0, 1.0, jnp.exp(jnp.minimum(v, 0.0)))


def forward_kernel(
    me_ref, slots_ref, degree_ref, table_ref, arrived_ref, cot_ref, w1_hbm, w2_hbm,
    joined_ref, pre_ref, hidden_two_ref, grad_two_ref, keep_ref, send_ref,
    wide, chosen, summed, hidden, w1_ref, w2_ref, w1_sem, w2_sem,
):
    load_one = pltpu.make_async_copy(w1_hbm, w1_ref, w1_sem)
    load_two = pltpu.make_async_copy(w2_hbm, w2_ref, w2_sem)
    load_one.start()
    load_two.start()
    widen(arrived_ref, wide, TABLE)
    wide[TABLE : TABLE + 8, :] = jnp.zeros((8, F), f32)

    for node in range(M1):
        wanted = [slots_ref[k, node] for k in range(16)]
        chosen[node : node + 1, :] = wide[pl.ds(wanted[15], 1), :]
        terms = [wide[pl.ds(wanted[k], 1), :] for k in range(FAN1)]
        while len(terms) > 1:
            pairs = [a + b for a, b in zip(terms[::2], terms[1::2])]
            terms = pairs + ([terms[-1]] if len(terms) % 2 else [])
        summed[node : node + 1, :] = terms[0]

    load_one.wait()
    for block in range(M1 // 128):
        rows = slice(block * 128, block * 128 + 128)
        degree = as_column(degree_ref[block : block + 1, :])
        joined_ref[rows, :F] = chosen[rows, :].astype(bf16)
        joined_ref[rows, F:] = (summed[rows, :] / degree).astype(bf16)
        pre = jnp.dot(joined_ref[rows, :], w1_ref[...], preferred_element_type=f32)
        pre_ref[rows, :] = pre
        hidden[rows, :] = elu(pre).astype(bf16)

    table = table_ref[...]
    onehot, counts = slot_counts(table)
    own = over_rows(onehot, hidden[...]).astype(bf16)
    degree = as_column(table[11:12, :])
    mean = (over_rows(counts, hidden[...]) / jnp.tile(degree, (1, H // 128))).astype(bf16)
    load_two.wait()
    pre_two = jnp.dot(own, w2_ref[:H, :], preferred_element_type=f32) + jnp.dot(
        mean, w2_ref[H:, :], preferred_element_type=f32
    )
    hidden_two_ref[...] = elu(pre_two).astype(bf16)
    grad_two_ref[...] = (cot_ref[...].astype(f32) * slope(pre_two)).astype(bf16)
    first = me_ref[0] // PEERS % 2 == 0

    @pl.when(first)
    def _():
        keep_ref[...] = own
        send_ref[...] = mean

    @pl.when(jnp.logical_not(first))
    def _():
        keep_ref[...] = mean
        send_ref[...] = own


def forward(me, slots, degree, table, arrived, cot, w1, w2):
    return pl.pallas_call(
        forward_kernel,
        name="forward",
        out_shape=(
            shape((M1, 2 * F), bf16),
            shape((M1, H), f32),
            shape((M2, H), bf16),
            shape((M2, H), bf16),
            shape((M2, H), bf16),
            shape((M2, H), bf16),
        ),
        in_specs=[SMEM, SMEM] + [VMEM] * 4 + [HBM, HBM],
        out_specs=[VMEM] * 6,
        scratch_shapes=[
            pltpu.VMEM((TABLE + 8, F), f32),
            pltpu.VMEM((M1, F), f32),
            pltpu.VMEM((M1, F), f32),
            pltpu.VMEM((M1, H), bf16),
            pltpu.VMEM((2 * F, H), bf16),
            pltpu.VMEM((2 * H, H), bf16),
            pltpu.SemaphoreType.DMA,
            pltpu.SemaphoreType.DMA,
        ],
        compiler_params=limit(20),
        cost_estimate=pl.CostEstimate(flops=1 << 30, bytes_accessed=10 << 20, transcendentals=1 << 19),
    )(me, slots, degree, table, arrived, cot, w1, w2)


def backward_kernel(table_ref, grad_two_ref, w2_ref, pre_ref, joined_ref, out_ref, stacked, spread, grad_pre):
    table = table_ref[...]
    grad_two = grad_two_ref[...]
    onehot, counts = slot_counts(table)
    stacked[:, :128] = onehot
    stacked[:, 128:256] = counts
    stacked[:, 256:] = counts
    dims = (((1,), (1,)), ((), ()))
    spread[:128, :] = lax.dot_general(grad_two, w2_ref[:H, :], dims, preferred_element_type=f32).astype(bf16)
    mean_grad = lax.dot_general(grad_two, w2_ref[H:, :], dims, preferred_element_type=f32).astype(bf16)
    degree = as_column(table[11:12, :])
    scaled = mean_grad.astype(f32) / jnp.tile(degree, (1, H // 128))
    high = scaled.astype(bf16)
    spread[128:256, :] = high
    spread[256:, :] = (scaled - high.astype(f32)).astype(bf16)
    for block in range(M1 // 128):
        rows = slice(block * 128, block * 128 + 128)
        grad_hidden = jnp.dot(stacked[rows, :], spread[...], preferred_element_type=f32).astype(bf16)
        grad_pre[rows, :] = (grad_hidden.astype(f32) * slope(pre_ref[rows, :])).astype(bf16)
    grad_one = over_rows(grad_pre[...], joined_ref[...]).astype(bf16)
    for xh in range(2):
        for rest in range(8):
            out_ref[xh * 8 + rest] = grad_one[rest * 128 : rest * 128 + 128, xh * 128 : xh * 128 + 128]


def backward(table, grad_two, w2, pre, joined):
    return pl.pallas_call(
        backward_kernel,
        name="backward",
        out_shape=shape((16, 128, 128), bf16),
        in_specs=[VMEM] * 5,
        out_specs=VMEM,
        scratch_shapes=[
            pltpu.VMEM((M1, 384), bf16),
            pltpu.VMEM((384, H), bf16),
            pltpu.VMEM((M1, H), bf16),
        ],
        compiler_params=limit(20),
        cost_estimate=pl.CostEstimate(flops=1 << 30, bytes_accessed=8 << 20, transcendentals=1 << 19),
    )(table, grad_two, w2, pre, joined)


def place_of(me, xh, xl, y):
    swapped = me // PEERS % 2 == 0

    def split(target, half):
        near, far = (target // 2 + target % 2 + half) % 2, target // 2
        return jnp.where(swapped, near, far), jnp.where(swapped, far, target % 2)

    outer_x, inner_x = split(xh * 2 + xl, me // 128)
    outer_y, inner_y = split(y, me // 16 % 2)
    return (outer_x * 2 + outer_y) * 2, (inner_x * 2 + inner_y) * 4


def product_kernel(me_ref, mine_ref, theirs_ref, keep_ref, got_ref, one_ref, out_ref):
    for rest in range(8):
        rows = slice(rest * 128, rest * 128 + 128)
        product = over_rows(mine_ref[:, rows], keep_ref[...]) + over_rows(theirs_ref[:, rows], got_ref[...])
        product = product.astype(bf16)
        for xh in range(2):
            outer, inner = place_of(me_ref[0], xh, rest // 4, rest % 4)
            one = one_ref[xh * 8 + rest]
            for z in range(8):
                rows = slice(z * 16, z * 16 + 16)
                for block in range(4):
                    column = (xh * 4 + block) * 128
                    out_ref[outer + z % 2, inner + z // 2, block] = product[rows, column : column + 128]
                out_ref[outer + z % 2, inner + z // 2, 4] = one[rows, :]


def product(me, mine, theirs, keep, got, one):
    return pl.pallas_call(
        product_kernel,
        name="product",
        out_shape=shape((8, 16, 5, 16, 128), bf16),
        in_specs=[SMEM] + [VMEM] * 5,
        out_specs=VMEM,
        compiler_params=limit(10),
        cost_estimate=pl.CostEstimate(flops=1 << 29, bytes_accessed=4 << 20, transcendentals=0),
    )(me, mine, theirs, keep, got, one)


def sum_kernel(parts_ref, out_ref):
    def total(first, count):
        if count == 1:
            return parts_ref[first].astype(f32)
        half = count // 2
        return total(first, half) + total(first + half, half)

    out_ref[...] = total(0, parts_ref.shape[0]).astype(out_ref.dtype)


def summed_parts(parts, dtype):
    return pl.pallas_call(
        sum_kernel,
        name="summed_parts",
        out_shape=shape(parts.shape[1:], dtype),
        in_specs=[VMEM],
        out_specs=VMEM,
        compiler_params=limit(8),
    )(parts)


def place_kernel(me_ref, mine_ref, core_ref, xh_ref, both_ref, one_ref, two_ref):
    my_xh, my_core = me_ref[0] // 128, me_ref[0] // PEERS % 2

    def piece(xh, core, block):
        same = jnp.where(my_core == core, mine_ref[block], core_ref[block])
        other = jnp.where(my_core == core, xh_ref[block], both_ref[block])
        return jnp.where(my_xh == xh, same, other)

    for xh in range(2):
        one_ref[:, xh * F : xh * F + F] = piece(xh, 0, 4) + piece(xh, 1, 4)
        for core in range(2):
            for block in range(4):
                column = core * H + xh * 512 + block * 128
                two_ref[:, column : column + 128] = piece(xh, core, block)


def placed(me, mine, core, xh, both):
    return pl.pallas_call(
        place_kernel,
        name="placed",
        out_shape=(shape((16, 2 * F), f32), shape((16, 2 * H), f32)),
        in_specs=[SMEM] + [VMEM] * 4,
        out_specs=[VMEM] * 2,
        compiler_params=limit(4),
    )(me, mine, core, xh, both)


def flat(xh, core, xl, y, z):
    return ((((xh * 2 + core) * 2 + xl) * 4 + y) * 8) + z


def in_section(device, steps):
    return (device + steps * PEERS) % DEVICES


def other_core(device):
    return device ^ 64


def other_xh(device):
    return device ^ 128


def permuted(value, target):
    return lax.ppermute(value, ALL, [(device, target(device)) for device in range(DEVICES)])


DEV_GROUPS = [[section * PEERS + peer for peer in range(PEERS)] for section in range(4)]
PAIRS = (((0, 1), (2, 3)), ((0, 3), (1, 2)))


def cubes():
    groups = []
    for core in range(2):
        for along_x in PAIRS[core]:
            for along_y in PAIRS[core]:
                for even in range(0, 8, 2):
                    along_z = (even, (even - 1 if core else even + 1) % 8)
                    groups.append([flat(x // 2, core, x % 2, y, z) for x in along_x for y in along_y for z in along_z])
    return groups


def rests():
    groups = []
    for core in range(2):
        for along_x in PAIRS[1 - core]:
            for along_y in PAIRS[1 - core]:
                for parity in range(2):
                    along_z = range(parity, 8, 2)
                    groups.append([flat(x // 2, core, x % 2, y, z) for x in along_x for y in along_y for z in along_z])
    return groups


def exchanged(value, groups):
    return lax.all_to_all(value, ALL, 0, 0, axis_index_groups=groups, tiled=True)


def per_device(
    feature_store, send_rows, send_counts, target_one, neighbor_one, degree_one,
    target_two, neighbor_two, degree_two, weight_one, weight_two, cotangent,
):
    me = lax.axis_index(ALL).astype(jnp.int32).reshape(1)
    slots, table = tables(neighbor_one, degree_one, target_one, neighbor_two, degree_two, target_two)
    table = permuted(table, lambda device: in_section(device, -1))
    cot = permuted(cotangent, lambda device: in_section(device, -1))

    outgoing = pick_rows(
        pltpu.with_memory_space_constraint(send_rows, pltpu.HBM),
        pltpu.with_memory_space_constraint(feature_store, pltpu.HBM),
    ).reshape(PEERS, CAP, F)
    arrived = exchanged(outgoing, DEV_GROUPS).reshape(TABLE, F)

    joined, pre, hidden_two, grad_two, keep, send = forward(
        me, slots, degree_one.reshape(4, 128), table, arrived, cot,
        pltpu.with_memory_space_constraint(weight_one, pltpu.HBM),
        pltpu.with_memory_space_constraint(weight_two, pltpu.HBM),
    )
    theirs = permuted(grad_two, other_core)
    got = permuted(send, other_core)
    hidden_two = pltpu.with_memory_space_constraint(
        permuted(hidden_two, lambda device: in_section(device, 1)), pltpu.HBM
    )
    one = backward(table, grad_two, weight_two, pre, joined)
    parts = product(me, grad_two, theirs, keep, got, one)

    parts = summed_parts(exchanged(parts, cubes()), bf16)
    mine = summed_parts(exchanged(parts, rests()), f32)
    from_core = permuted(mine, other_core)
    from_xh = permuted(mine, other_xh)
    from_both = permuted(from_core, other_xh)
    grad_one_out, grad_two_out = placed(me, mine, from_core, from_xh, from_both)
    return hidden_two, grad_one_out, grad_two_out


def solution(mesh):
    return jax.shard_map(
        per_device,
        mesh=mesh,
        in_specs=(
            P(ALL, None), P(ALL, None), P(ALL), P(ALL), P(None, ALL), P(ALL),
            P(ALL), P(None, ALL), P(ALL), P(), P(), P(ALL, None),
        ),
        out_specs=(P(ALL, None), P("dev", None), P("dev", None)),
        check_vma=False,
    )
```

```python
import jax
import jax.numpy as jnp
from jax import lax
from jax.experimental import pallas as pl
from jax.experimental.pallas import tpu as pltpu
from jax.sharding import PartitionSpec as P


F = 128
H = 1024
FAN1 = 15
FAN2 = 10
CAP = 64
STORE_ROWS = 4096
M2 = 128
M1 = 512
PEERS = 64
TABLE = PEERS * CAP
DEVICES = 256
ALL = ("sec", "dev")

bf16 = jnp.bfloat16
f32 = jnp.float32
VMEM = pl.BlockSpec(memory_space=pltpu.VMEM)
SMEM = pl.BlockSpec(memory_space=pltpu.SMEM)
HBM = pl.BlockSpec(memory_space=pltpu.HBM)


def limit(mib):
    return pltpu.CompilerParams(vmem_limit_bytes=mib * 1024 * 1024)


def shape(dims, dtype):
    return jax.ShapeDtypeStruct(dims, dtype)


def widen(source, wide, rows):
    def chunk(step, carry):
        here = pl.ds(pl.multiple_of(step * 256, 256), 256)
        wide[here, :] = source[here, :].astype(f32)
        return carry

    lax.fori_loop(0, rows // 256, chunk, 0)


def pick_kernel(rows_ref, store_ref, out_ref, wide, picked):
    widen(store_ref, wide, STORE_ROWS)

    for peer in range(PEERS):
        base = peer * CAP
        for slot in range(CAP):
            picked[base + slot : base + slot + 1, :] = wide[pl.ds(rows_ref[peer, slot], 1), :]
        out_ref[base : base + CAP, :] = picked[base : base + CAP, :].astype(bf16)


def pick_rows(send_rows, store):
    return pl.pallas_call(
        pick_kernel,
        name="pick_rows",
        out_shape=shape((TABLE, F), bf16),
        in_specs=[SMEM, VMEM],
        out_specs=VMEM,
        scratch_shapes=[pltpu.VMEM((STORE_ROWS, F), f32), pltpu.VMEM((TABLE, F), f32)],
        compiler_params=limit(10),
        cost_estimate=pl.CostEstimate(flops=0, bytes_accessed=2 << 20, transcendentals=0),
    )(send_rows, store)


def table_kernel(n2_ref, d2_ref, t2_ref, table_ref):
    table_ref[:FAN2, :] = n2_ref[...]
    table_ref[FAN2 : FAN2 + 1, :] = t2_ref[...]
    table_ref[FAN2 + 1 : FAN2 + 2, :] = d2_ref[...]
    table_ref[FAN2 + 2 :, :] = jnp.zeros((14 - FAN2, M2), jnp.int32)


def packed_table(n2, d2, t2):
    return pl.pallas_call(
        table_kernel,
        name="packed_table",
        out_shape=shape((16, M2), jnp.int32),
        in_specs=[VMEM] * 3,
        out_specs=VMEM,
        compiler_params=limit(2),
    )(n2, d2.reshape(1, M2), t2.reshape(1, M2))


def matrix_kernel(n1_ref, d1_ref, counts_ref, block, lane):
    order = lax.broadcasted_iota(jnp.int32, (FAN1, M1), 0)
    live = order < d1_ref[...]
    row = n1_ref[...]
    block[...] = jnp.where(live, row // 128, -1).astype(f32).T
    lane[...] = (row % 128).astype(f32).T
    lanes = lax.broadcasted_iota(jnp.int32, (16, 128), 1).astype(bf16)
    zero, one = jnp.zeros((16, 128), bf16), jnp.ones((16, 128), bf16)

    def sixteen_nodes(step, carry):
        rows = pl.ds(pl.multiple_of(step * 16, 16), 16)
        blocks = [jnp.broadcast_to(block[rows, k : k + 1], (16, 128)).astype(bf16) for k in range(FAN1)]
        hits = [
            jnp.where(jnp.broadcast_to(lane[rows, k : k + 1], (16, 128)).astype(bf16) == lanes, one, zero)
            for k in range(FAN1)
        ]
        for tile in range(TABLE // 128):
            columns = slice(tile * 128, tile * 128 + 128)
            terms = [jnp.where(blocks[k] == bf16(tile), hits[k], zero) for k in range(FAN1)]
            while len(terms) > 1:
                pairs = [a + b for a, b in zip(terms[::2], terms[1::2])]
                terms = pairs + ([terms[-1]] if len(terms) % 2 else [])
            counts_ref[rows, columns] = terms[0]
        return carry

    lax.fori_loop(0, M1 // 16, sixteen_nodes, 0)


def count_matrix(n1, d1):
    return pl.pallas_call(
        matrix_kernel,
        name="count_matrix",
        out_shape=shape((M1, TABLE), bf16),
        in_specs=[VMEM] * 2,
        out_specs=VMEM,
        scratch_shapes=[pltpu.VMEM((M1, FAN1), f32), pltpu.VMEM((M1, FAN1), f32)],
        compiler_params=limit(8),
        cost_estimate=pl.CostEstimate(flops=1 << 27, bytes_accessed=4 << 20, transcendentals=0),
    )(n1, d1.reshape(1, M1))


def as_column(row):
    return jnp.broadcast_to(row.astype(f32), (128, 128)).T


def slot_counts(table):
    places = lax.broadcasted_iota(jnp.int32, (M1, M2), 0)
    degree = table[11:12, :]
    counts = jnp.zeros((M1, M2), f32)
    for k in range(FAN2):
        live = (places == table[k : k + 1, :]) & (degree > k)
        counts = counts + live.astype(f32)
    chosen = (places == table[10:11, :]).astype(f32)
    return chosen.astype(bf16), counts.astype(bf16)


def over_rows(a, b):
    return lax.dot_general(a, b, (((0,), (0,)), ((), ())), preferred_element_type=f32)


def elu(v):
    return jnp.where(v > 0, v, jnp.exp(jnp.minimum(v, 0.0)) - 1.0)


def slope(v):
    return jnp.where(v > 0, 1.0, jnp.exp(jnp.minimum(v, 0.0)))


def forward_kernel(
    me_ref, targets_ref, degree_ref, table_ref, arrived_ref, cot_ref, counts_hbm, w1_hbm, w2_hbm,
    joined_ref, pre_ref, hidden_two_ref, grad_two_ref, keep_ref, send_ref,
    wide, chosen, hidden, counts_ref, w1_ref, w2_ref, counts_sem, w1_sem, w2_sem,
):
    loads = []
    for half in range(2):
        rows = pl.ds(half * M1 // 2, M1 // 2)
        loads.append(pltpu.make_async_copy(counts_hbm.at[rows], counts_ref.at[rows], counts_sem.at[half]))
    load_one = pltpu.make_async_copy(w1_hbm, w1_ref, w1_sem)
    load_two = pltpu.make_async_copy(w2_hbm, w2_ref, w2_sem)
    for load in loads + [load_one, load_two]:
        load.start()
    widen(arrived_ref, wide, TABLE)
    for node in range(M1):
        chosen[node : node + 1, :] = wide[pl.ds(targets_ref[node], 1), :]
    for half in range(2):
        rows = slice(half * M1 // 2, half * M1 // 2 + M1 // 2)
        loads[half].wait()
        summed = jnp.dot(counts_ref[rows, :], arrived_ref[...], preferred_element_type=f32)
        degree = jnp.concatenate([as_column(degree_ref[block : block + 1, :]) for block in (half * 2, half * 2 + 1)])
        joined_ref[rows, :F] = chosen[rows, :].astype(bf16)
        joined_ref[rows, F:] = (summed / degree).astype(bf16)
    load_one.wait()
    for block in range(M1 // 128):
        rows = slice(block * 128, block * 128 + 128)
        pre = jnp.dot(joined_ref[rows, :], w1_ref[...], preferred_element_type=f32)
        pre_ref[rows, :] = pre
        hidden[rows, :] = elu(pre).astype(bf16)

    table = table_ref[...]
    onehot, counts = slot_counts(table)
    own = over_rows(onehot, hidden[...]).astype(bf16)
    degree = as_column(table[11:12, :])
    mean = (over_rows(counts, hidden[...]) / jnp.tile(degree, (1, H // 128))).astype(bf16)
    load_two.wait()
    pre_two = jnp.dot(own, w2_ref[:H, :], preferred_element_type=f32) + jnp.dot(
        mean, w2_ref[H:, :], preferred_element_type=f32
    )
    hidden_two_ref[...] = elu(pre_two).astype(bf16)
    grad_two_ref[...] = (cot_ref[...].astype(f32) * slope(pre_two)).astype(bf16)
    first = me_ref[0] // PEERS % 2 == 0

    @pl.when(first)
    def _():
        keep_ref[...] = own
        send_ref[...] = mean

    @pl.when(jnp.logical_not(first))
    def _():
        keep_ref[...] = mean
        send_ref[...] = own


def forward(me, targets, degree, table, arrived, cot, counts, w1, w2):
    return pl.pallas_call(
        forward_kernel,
        name="forward",
        out_shape=(
            shape((M1, 2 * F), bf16),
            shape((M1, H), f32),
            shape((M2, H), bf16),
            shape((M2, H), bf16),
            shape((M2, H), bf16),
            shape((M2, H), bf16),
        ),
        in_specs=[SMEM, SMEM] + [VMEM] * 4 + [HBM] * 3,
        out_specs=[VMEM] * 6,
        scratch_shapes=[
            pltpu.VMEM((TABLE, F), f32),
            pltpu.VMEM((M1, F), f32),
            pltpu.VMEM((M1, H), bf16),
            pltpu.VMEM((M1, TABLE), bf16),
            pltpu.VMEM((2 * F, H), bf16),
            pltpu.VMEM((2 * H, H), bf16),
            pltpu.SemaphoreType.DMA((2,)),
            pltpu.SemaphoreType.DMA,
            pltpu.SemaphoreType.DMA,
        ],
        compiler_params=limit(24),
        cost_estimate=pl.CostEstimate(flops=3 << 30, bytes_accessed=10 << 20, transcendentals=1 << 19),
    )(me, targets, degree, table, arrived, cot, counts, w1, w2)


def backward_kernel(table_ref, grad_two_ref, w2_ref, pre_ref, joined_ref, out_ref, stacked, spread, grad_pre):
    table = table_ref[...]
    grad_two = grad_two_ref[...]
    onehot, counts = slot_counts(table)
    stacked[:, :128] = onehot
    stacked[:, 128:256] = counts
    stacked[:, 256:] = counts
    dims = (((1,), (1,)), ((), ()))
    spread[:128, :] = lax.dot_general(grad_two, w2_ref[:H, :], dims, preferred_element_type=f32).astype(bf16)
    mean_grad = lax.dot_general(grad_two, w2_ref[H:, :], dims, preferred_element_type=f32).astype(bf16)
    degree = as_column(table[11:12, :])
    scaled = mean_grad.astype(f32) / jnp.tile(degree, (1, H // 128))
    high = scaled.astype(bf16)
    spread[128:256, :] = high
    spread[256:, :] = (scaled - high.astype(f32)).astype(bf16)
    for block in range(M1 // 128):
        rows = slice(block * 128, block * 128 + 128)
        grad_hidden = jnp.dot(stacked[rows, :], spread[...], preferred_element_type=f32).astype(bf16)
        grad_pre[rows, :] = (grad_hidden.astype(f32) * slope(pre_ref[rows, :])).astype(bf16)
    grad_one = over_rows(grad_pre[...], joined_ref[...]).astype(bf16)
    for xh in range(2):
        for rest in range(8):
            out_ref[xh * 8 + rest] = grad_one[rest * 128 : rest * 128 + 128, xh * 128 : xh * 128 + 128]


def backward(table, grad_two, w2, pre, joined):
    return pl.pallas_call(
        backward_kernel,
        name="backward",
        out_shape=shape((16, 128, 128), bf16),
        in_specs=[VMEM] * 5,
        out_specs=VMEM,
        scratch_shapes=[
            pltpu.VMEM((M1, 384), bf16),
            pltpu.VMEM((384, H), bf16),
            pltpu.VMEM((M1, H), bf16),
        ],
        compiler_params=limit(20),
        cost_estimate=pl.CostEstimate(flops=1 << 30, bytes_accessed=8 << 20, transcendentals=1 << 19),
    )(table, grad_two, w2, pre, joined)


def place_of(me, xh, xl, y):
    swapped = me // PEERS % 2 == 0

    def split(target, half):
        near, far = (target // 2 + target % 2 + half) % 2, target // 2
        return jnp.where(swapped, near, far), jnp.where(swapped, far, target % 2)

    outer_x, inner_x = split(xh * 2 + xl, me // 128)
    outer_y, inner_y = split(y, me // 16 % 2)
    return (outer_x * 2 + outer_y) * 2, (inner_x * 2 + inner_y) * 4


def product_kernel(me_ref, mine_ref, theirs_ref, keep_ref, got_ref, one_ref, out_ref):
    for rest in range(8):
        rows = slice(rest * 128, rest * 128 + 128)
        product = over_rows(mine_ref[:, rows], keep_ref[...]) + over_rows(theirs_ref[:, rows], got_ref[...])
        product = product.astype(bf16)
        for xh in range(2):
            outer, inner = place_of(me_ref[0], xh, rest // 4, rest % 4)
            one = one_ref[xh * 8 + rest]
            for z in range(8):
                rows = slice(z * 16, z * 16 + 16)
                for block in range(4):
                    column = (xh * 4 + block) * 128
                    out_ref[outer + z % 2, inner + z // 2, block] = product[rows, column : column + 128]
                out_ref[outer + z % 2, inner + z // 2, 4] = one[rows, :]


def product(me, mine, theirs, keep, got, one):
    return pl.pallas_call(
        product_kernel,
        name="product",
        out_shape=shape((8, 16, 5, 16, 128), bf16),
        in_specs=[SMEM] + [VMEM] * 5,
        out_specs=VMEM,
        compiler_params=limit(10),
        cost_estimate=pl.CostEstimate(flops=1 << 29, bytes_accessed=4 << 20, transcendentals=0),
    )(me, mine, theirs, keep, got, one)


def sum_kernel(parts_ref, out_ref):
    def total(first, count):
        if count == 1:
            return parts_ref[first].astype(f32)
        half = count // 2
        return total(first, half) + total(first + half, half)

    out_ref[...] = total(0, parts_ref.shape[0]).astype(out_ref.dtype)


def summed_parts(parts, dtype):
    return pl.pallas_call(
        sum_kernel,
        name="summed_parts",
        out_shape=shape(parts.shape[1:], dtype),
        in_specs=[VMEM],
        out_specs=VMEM,
        compiler_params=limit(8),
    )(parts)


def place_kernel(me_ref, mine_ref, core_ref, xh_ref, both_ref, hidden_ref, hidden_out, one_ref, two_ref):
    hidden_out[...] = hidden_ref[...]
    my_xh, my_core = me_ref[0] // 128, me_ref[0] // PEERS % 2

    def piece(xh, core, block):
        same = jnp.where(my_core == core, mine_ref[block], core_ref[block])
        other = jnp.where(my_core == core, xh_ref[block], both_ref[block])
        return jnp.where(my_xh == xh, same, other)

    for xh in range(2):
        one_ref[:, xh * F : xh * F + F] = piece(xh, 0, 4) + piece(xh, 1, 4)
        for core in range(2):
            for block in range(4):
                column = core * H + xh * 512 + block * 128
                two_ref[:, column : column + 128] = piece(xh, core, block)


def placed(me, mine, core, xh, both, hidden):
    return pl.pallas_call(
        place_kernel,
        name="placed",
        out_shape=(shape((M2, H), bf16), shape((16, 2 * F), f32), shape((16, 2 * H), f32)),
        in_specs=[SMEM] + [VMEM] * 5,
        out_specs=[VMEM] * 3,
        compiler_params=limit(4),
    )(me, mine, core, xh, both, hidden)


def flat(xh, core, xl, y, z):
    return ((((xh * 2 + core) * 2 + xl) * 4 + y) * 8) + z


def in_section(device, steps):
    return (device + steps * PEERS) % DEVICES


def other_core(device):
    return device ^ 64


def other_xh(device):
    return device ^ 128


def permuted(value, target):
    return lax.ppermute(value, ALL, [(device, target(device)) for device in range(DEVICES)])


DEV_GROUPS = [[section * PEERS + peer for peer in range(PEERS)] for section in range(4)]
PAIRS = (((0, 1), (2, 3)), ((0, 3), (1, 2)))


def cubes():
    groups = []
    for core in range(2):
        for along_x in PAIRS[core]:
            for along_y in PAIRS[core]:
                for even in range(0, 8, 2):
                    along_z = (even, (even - 1 if core else even + 1) % 8)
                    groups.append([flat(x // 2, core, x % 2, y, z) for x in along_x for y in along_y for z in along_z])
    return groups


def rests():
    groups = []
    for core in range(2):
        for along_x in PAIRS[1 - core]:
            for along_y in PAIRS[1 - core]:
                for parity in range(2):
                    along_z = range(parity, 8, 2)
                    groups.append([flat(x // 2, core, x % 2, y, z) for x in along_x for y in along_y for z in along_z])
    return groups


def exchanged(value, groups):
    return lax.all_to_all(value, ALL, 0, 0, axis_index_groups=groups, tiled=True)


def per_device(
    feature_store, send_rows, send_counts, target_one, neighbor_one, degree_one,
    target_two, neighbor_two, degree_two, weight_one, weight_two, cotangent,
):
    me = lax.axis_index(ALL).astype(jnp.int32).reshape(1)
    table = packed_table(neighbor_two, degree_two, target_two)
    table = permuted(table, lambda device: in_section(device, -1))
    cot = permuted(cotangent, lambda device: in_section(device, -1))

    outgoing = pick_rows(
        pltpu.with_memory_space_constraint(send_rows, pltpu.HBM),
        pltpu.with_memory_space_constraint(feature_store, pltpu.HBM),
    ).reshape(PEERS, CAP, F)
    arrived = exchanged(outgoing, DEV_GROUPS).reshape(TABLE, F)

    counts = count_matrix(neighbor_one, degree_one)
    joined, pre, hidden_two, grad_two, keep, send = forward(
        me, target_one, degree_one.reshape(4, 128), table, arrived, cot,
        *[pltpu.with_memory_space_constraint(value, pltpu.HBM) for value in (counts, weight_one, weight_two)],
    )
    theirs = permuted(grad_two, other_core)
    got = permuted(send, other_core)
    hidden_two = permuted(hidden_two, lambda device: in_section(device, 1))
    one = backward(table, grad_two, weight_two, pre, joined)
    parts = product(me, grad_two, theirs, keep, got, one)

    parts = summed_parts(exchanged(parts, cubes()), bf16)
    mine = summed_parts(exchanged(parts, rests()), f32)
    from_core = permuted(mine, other_core)
    from_xh = permuted(mine, other_xh)
    from_both = permuted(from_core, other_xh)
    return placed(me, mine, from_core, from_xh, from_both, hidden_two)


def solution(mesh):
    return jax.shard_map(
        per_device,
        mesh=mesh,
        in_specs=(
            P(ALL, None), P(ALL, None), P(ALL), P(ALL), P(None, ALL), P(ALL),
            P(ALL), P(None, ALL), P(ALL), P(), P(), P(ALL, None),
        ),
        out_specs=(P(ALL, None), P("dev", None), P("dev", None)),
        check_vma=False,
    )
```

```python
import jax
import jax.numpy as jnp
from jax import lax
from jax.experimental import pallas as pl
from jax.experimental.pallas import tpu as pltpu
from jax.sharding import PartitionSpec as P


F = 128
H = 1024
FAN1 = 15
FAN2 = 10
CAP = 64
STORE_ROWS = 4096
M2 = 128
M1 = 512
PEERS = 64
TABLE = PEERS * CAP
DEVICES = 256
ALL = ("sec", "dev")

bf16 = jnp.bfloat16
f32 = jnp.float32
VMEM = pl.BlockSpec(memory_space=pltpu.VMEM)
SMEM = pl.BlockSpec(memory_space=pltpu.SMEM)
HBM = pl.BlockSpec(memory_space=pltpu.HBM)


def limit(mib):
    return pltpu.CompilerParams(vmem_limit_bytes=mib * 1024 * 1024)


def shape(dims, dtype):
    return jax.ShapeDtypeStruct(dims, dtype)


def widen(source, wide, rows):
    def chunk(step, carry):
        here = pl.ds(pl.multiple_of(step * 256, 256), 256)
        wide[here, :] = source[here, :].astype(f32)
        return carry

    lax.fori_loop(0, rows // 256, chunk, 0)


QUARTER = TABLE // 4


def pick_kernel(rows_ref, store_hbm, out_hbm, store, wide, picked, packed, in_sems, out_sems):
    loads, saves = [], []
    for quarter in range(4):
        rows = pl.ds(quarter * QUARTER, QUARTER)
        loads.append(pltpu.make_async_copy(store_hbm.at[rows], store.at[rows], in_sems.at[quarter]))
        saves.append(pltpu.make_async_copy(packed.at[rows], out_hbm.at[rows], out_sems.at[quarter]))
        loads[quarter].start()
    for quarter in range(4):
        rows = slice(quarter * QUARTER, quarter * QUARTER + QUARTER)
        loads[quarter].wait()
        wide[rows, :] = store[rows, :].astype(f32)
    for quarter in range(4):
        for peer in range(quarter * PEERS // 4, (quarter + 1) * PEERS // 4):
            base = peer * CAP
            for slot in range(CAP):
                picked[base + slot : base + slot + 1, :] = wide[pl.ds(rows_ref[peer, slot], 1), :]
            packed[base : base + CAP, :] = picked[base : base + CAP, :].astype(bf16)
        saves[quarter].start()
    for quarter in range(4):
        saves[quarter].wait()


def pick_rows(send_rows, store):
    return pl.pallas_call(
        pick_kernel,
        name="pick_rows",
        out_shape=shape((TABLE, F), bf16),
        in_specs=[SMEM, HBM],
        out_specs=HBM,
        scratch_shapes=[
            pltpu.VMEM((STORE_ROWS, F), bf16),
            pltpu.VMEM((STORE_ROWS, F), f32),
            pltpu.VMEM((TABLE, F), f32),
            pltpu.VMEM((TABLE, F), bf16),
            pltpu.SemaphoreType.DMA((4,)),
            pltpu.SemaphoreType.DMA((4,)),
        ],
        compiler_params=limit(10),
        cost_estimate=pl.CostEstimate(flops=0, bytes_accessed=2 << 20, transcendentals=0),
    )(send_rows, store)


def table_kernel(n2_ref, d2_ref, t2_ref, table_ref):
    table_ref[:FAN2, :] = n2_ref[...]
    table_ref[FAN2 : FAN2 + 1, :] = t2_ref[...]
    table_ref[FAN2 + 1 : FAN2 + 2, :] = d2_ref[...]
    table_ref[FAN2 + 2 :, :] = jnp.zeros((14 - FAN2, M2), jnp.int32)


def packed_table(n2, d2, t2):
    return pl.pallas_call(
        table_kernel,
        name="packed_table",
        out_shape=shape((16, M2), jnp.int32),
        in_specs=[VMEM] * 3,
        out_specs=VMEM,
        compiler_params=limit(2),
    )(n2, d2.reshape(1, M2), t2.reshape(1, M2))


def matrix_kernel(n1_ref, d1_ref, counts_ref, block, lane):
    order = lax.broadcasted_iota(jnp.int32, (FAN1, M1), 0)
    live = order < d1_ref[...]
    row = n1_ref[...]
    block[...] = jnp.where(live, row // 128, -1).astype(f32).T
    lane[...] = (row % 128).astype(f32).T
    lanes = lax.broadcasted_iota(jnp.int32, (16, 128), 1).astype(bf16)
    zero, one = jnp.zeros((16, 128), bf16), jnp.ones((16, 128), bf16)

    def sixteen_nodes(step, carry):
        rows = pl.ds(pl.multiple_of(step * 16, 16), 16)
        blocks = [jnp.broadcast_to(block[rows, k : k + 1], (16, 128)).astype(bf16) for k in range(FAN1)]
        hits = [
            jnp.where(jnp.broadcast_to(lane[rows, k : k + 1], (16, 128)).astype(bf16) == lanes, one, zero)
            for k in range(FAN1)
        ]
        for tile in range(TABLE // 128):
            columns = slice(tile * 128, tile * 128 + 128)
            terms = [jnp.where(blocks[k] == bf16(tile), hits[k], zero) for k in range(FAN1)]
            while len(terms) > 1:
                pairs = [a + b for a, b in zip(terms[::2], terms[1::2])]
                terms = pairs + ([terms[-1]] if len(terms) % 2 else [])
            counts_ref[rows, columns] = terms[0]
        return carry

    lax.fori_loop(0, M1 // 16, sixteen_nodes, 0)


def count_matrix(n1, d1):
    return pl.pallas_call(
        matrix_kernel,
        name="count_matrix",
        out_shape=shape((M1, TABLE), bf16),
        in_specs=[VMEM] * 2,
        out_specs=VMEM,
        scratch_shapes=[pltpu.VMEM((M1, FAN1), f32), pltpu.VMEM((M1, FAN1), f32)],
        compiler_params=limit(8),
        cost_estimate=pl.CostEstimate(flops=1 << 27, bytes_accessed=4 << 20, transcendentals=0),
    )(n1, d1.reshape(1, M1))


def as_column(row):
    return jnp.broadcast_to(row.astype(f32), (128, 128)).T


def slot_counts(table):
    places = lax.broadcasted_iota(jnp.int32, (M1, M2), 0)
    degree = table[11:12, :]
    counts = jnp.zeros((M1, M2), f32)
    for k in range(FAN2):
        live = (places == table[k : k + 1, :]) & (degree > k)
        counts = counts + live.astype(f32)
    chosen = (places == table[10:11, :]).astype(f32)
    return chosen.astype(bf16), counts.astype(bf16)


def over_rows(a, b):
    return lax.dot_general(a, b, (((0,), (0,)), ((), ())), preferred_element_type=f32)


def elu(v):
    return jnp.where(v > 0, v, jnp.exp(jnp.minimum(v, 0.0)) - 1.0)


def slope(v):
    return jnp.where(v > 0, 1.0, jnp.exp(jnp.minimum(v, 0.0)))


def forward_kernel(
    me_ref, targets_ref, degree_ref, table_ref, arrived_ref, cot_ref, counts_hbm, w1_hbm, w2_hbm,
    joined_ref, pre_ref, hidden_two_ref, grad_two_ref, keep_ref, send_ref, w2_ref,
    wide, chosen, hidden, counts_ref, w1_ref, counts_sem, w1_sem, w2_sem,
):
    loads = []
    for half in range(2):
        rows = pl.ds(half * M1 // 2, M1 // 2)
        loads.append(pltpu.make_async_copy(counts_hbm.at[rows], counts_ref.at[rows], counts_sem.at[half]))
    load_one = pltpu.make_async_copy(w1_hbm, w1_ref, w1_sem)
    load_two = pltpu.make_async_copy(w2_hbm, w2_ref, w2_sem)
    for load in loads + [load_one, load_two]:
        load.start()
    widen(arrived_ref, wide, TABLE)
    for node in range(M1):
        chosen[node : node + 1, :] = wide[pl.ds(targets_ref[node], 1), :]
    for half in range(2):
        rows = slice(half * M1 // 2, half * M1 // 2 + M1 // 2)
        loads[half].wait()
        summed = jnp.dot(counts_ref[rows, :], arrived_ref[...], preferred_element_type=f32)
        degree = jnp.concatenate([as_column(degree_ref[block : block + 1, :]) for block in (half * 2, half * 2 + 1)])
        joined_ref[rows, :F] = chosen[rows, :].astype(bf16)
        joined_ref[rows, F:] = (summed / degree).astype(bf16)
    load_one.wait()
    for block in range(M1 // 128):
        rows = slice(block * 128, block * 128 + 128)
        pre = jnp.dot(joined_ref[rows, :], w1_ref[...], preferred_element_type=f32)
        pre_ref[rows, :] = pre
        hidden[rows, :] = elu(pre).astype(bf16)

    table = table_ref[...]
    onehot, counts = slot_counts(table)
    own = over_rows(onehot, hidden[...]).astype(bf16)
    degree = as_column(table[11:12, :])
    mean = (over_rows(counts, hidden[...]) / jnp.tile(degree, (1, H // 128))).astype(bf16)
    load_two.wait()
    pre_two = jnp.dot(own, w2_ref[:H, :], preferred_element_type=f32) + jnp.dot(
        mean, w2_ref[H:, :], preferred_element_type=f32
    )
    hidden_two_ref[...] = elu(pre_two).astype(bf16)
    grad_two_ref[...] = (cot_ref[...].astype(f32) * slope(pre_two)).astype(bf16)
    first = me_ref[0] // PEERS % 2 == 0

    @pl.when(first)
    def _():
        keep_ref[...] = own
        send_ref[...] = mean

    @pl.when(jnp.logical_not(first))
    def _():
        keep_ref[...] = mean
        send_ref[...] = own


def forward(me, targets, degree, table, arrived, cot, counts, w1, w2):
    return pl.pallas_call(
        forward_kernel,
        name="forward",
        out_shape=(
            shape((M1, 2 * F), bf16),
            shape((M1, H), f32),
            shape((M2, H), bf16),
            shape((M2, H), bf16),
            shape((M2, H), bf16),
            shape((M2, H), bf16),
            shape((2 * H, H), bf16),
        ),
        in_specs=[SMEM, SMEM] + [VMEM] * 4 + [HBM] * 3,
        out_specs=[VMEM] * 7,
        scratch_shapes=[
            pltpu.VMEM((TABLE, F), f32),
            pltpu.VMEM((M1, F), f32),
            pltpu.VMEM((M1, H), bf16),
            pltpu.VMEM((M1, TABLE), bf16),
            pltpu.VMEM((2 * F, H), bf16),
            pltpu.SemaphoreType.DMA((2,)),
            pltpu.SemaphoreType.DMA,
            pltpu.SemaphoreType.DMA,
        ],
        compiler_params=limit(24),
        cost_estimate=pl.CostEstimate(flops=3 << 30, bytes_accessed=10 << 20, transcendentals=1 << 19),
    )(me, targets, degree, table, arrived, cot, counts, w1, w2)


def backward_kernel(table_ref, grad_two_ref, w2_ref, pre_ref, joined_ref, out_ref, stacked, spread, grad_pre):
    table = table_ref[...]
    grad_two = grad_two_ref[...]
    onehot, counts = slot_counts(table)
    stacked[:, :128] = onehot
    stacked[:, 128:256] = counts
    stacked[:, 256:] = counts
    dims = (((1,), (1,)), ((), ()))
    spread[:128, :] = lax.dot_general(grad_two, w2_ref[:H, :], dims, preferred_element_type=f32).astype(bf16)
    mean_grad = lax.dot_general(grad_two, w2_ref[H:, :], dims, preferred_element_type=f32).astype(bf16)
    degree = as_column(table[11:12, :])
    scaled = mean_grad.astype(f32) / jnp.tile(degree, (1, H // 128))
    high = scaled.astype(bf16)
    spread[128:256, :] = high
    spread[256:, :] = (scaled - high.astype(f32)).astype(bf16)
    for block in range(M1 // 128):
        rows = slice(block * 128, block * 128 + 128)
        grad_hidden = jnp.dot(stacked[rows, :], spread[...], preferred_element_type=f32).astype(bf16)
        grad_pre[rows, :] = (grad_hidden.astype(f32) * slope(pre_ref[rows, :])).astype(bf16)
    grad_one = over_rows(grad_pre[...], joined_ref[...]).astype(bf16)
    for xh in range(2):
        for rest in range(8):
            out_ref[xh * 8 + rest] = grad_one[rest * 128 : rest * 128 + 128, xh * 128 : xh * 128 + 128]


def backward(table, grad_two, w2, pre, joined):
    return pl.pallas_call(
        backward_kernel,
        name="backward",
        out_shape=shape((16, 128, 128), bf16),
        in_specs=[VMEM] * 5,
        out_specs=VMEM,
        scratch_shapes=[
            pltpu.VMEM((M1, 384), bf16),
            pltpu.VMEM((384, H), bf16),
            pltpu.VMEM((M1, H), bf16),
        ],
        compiler_params=limit(20),
        cost_estimate=pl.CostEstimate(flops=1 << 30, bytes_accessed=8 << 20, transcendentals=1 << 19),
    )(table, grad_two, w2, pre, joined)


def place_of(me, xh, xl, y):
    swapped = me // PEERS % 2 == 0

    def split(target, half):
        near, far = (target // 2 + target % 2 + half) % 2, target // 2
        return jnp.where(swapped, near, far), jnp.where(swapped, far, target % 2)

    outer_x, inner_x = split(xh * 2 + xl, me // 128)
    outer_y, inner_y = split(y, me // 16 % 2)
    return (outer_x * 2 + outer_y) * 2, (inner_x * 2 + inner_y) * 4, [split(ring, 0) for ring in range(4)]


def product_kernel(me_ref, mine_ref, theirs_ref, keep_ref, got_ref, one_ref, out_ref):
    for rest in range(8):
        rows = slice(rest * 128, rest * 128 + 128)
        product = over_rows(mine_ref[:, rows], keep_ref[...]) + over_rows(theirs_ref[:, rows], got_ref[...])
        product = product.astype(bf16)
        for xh in range(2):
            outer, inner, along_z = place_of(me_ref[0], xh, rest // 4, rest % 4)
            one = one_ref[xh * 8 + rest]
            for z in range(8):
                rows = slice(z * 16, z * 16 + 16)
                group = outer + along_z[z % 4][0]
                part = inner + along_z[z % 4][1] * 2 + z // 4
                for block in range(4):
                    column = (xh * 4 + block) * 128
                    out_ref[group, part, block] = product[rows, column : column + 128]
                out_ref[group, part, 4] = one[rows, :]


def product(me, mine, theirs, keep, got, one):
    return pl.pallas_call(
        product_kernel,
        name="product",
        out_shape=shape((8, 16, 5, 16, 128), bf16),
        in_specs=[SMEM] + [VMEM] * 5,
        out_specs=VMEM,
        compiler_params=limit(10),
        cost_estimate=pl.CostEstimate(flops=1 << 29, bytes_accessed=4 << 20, transcendentals=0),
    )(me, mine, theirs, keep, got, one)


def sum_kernel(parts_ref, out_ref):
    def total(first, count):
        if count == 1:
            return parts_ref[first].astype(f32)
        half = count // 2
        return total(first, half) + total(first + half, half)

    out_ref[...] = total(0, parts_ref.shape[0]).astype(out_ref.dtype)


def summed_parts(parts):
    return pl.pallas_call(
        sum_kernel,
        name="summed_parts",
        out_shape=shape(parts.shape[1:], bf16),
        in_specs=[VMEM],
        out_specs=VMEM,
        compiler_params=limit(8),
    )(parts)


def spread_kernel(parts_ref, out_ref, total):
    sum_kernel(parts_ref, total)
    for section in range(4):
        out_ref[section] = total[...]


def spread_parts(parts):
    return pl.pallas_call(
        spread_kernel,
        name="spread_parts",
        out_shape=shape((4,) + parts.shape[1:], bf16),
        in_specs=[VMEM],
        out_specs=VMEM,
        scratch_shapes=[pltpu.VMEM(parts.shape[1:], bf16)],
        compiler_params=limit(4),
    )(parts)


def place_kernel(parts_ref, hidden_ref, hidden_out, one_ref, two_ref):
    hidden_out[...] = hidden_ref[...]

    def piece(xh, core, block):
        section = xh * 2 + core
        return parts_ref[section, 0, block].astype(f32) + parts_ref[section, 1, block].astype(f32)

    for xh in range(2):
        one_ref[:, xh * F : xh * F + F] = piece(xh, 0, 4) + piece(xh, 1, 4)
        for core in range(2):
            for block in range(4):
                column = core * H + xh * 512 + block * 128
                two_ref[:, column : column + 128] = piece(xh, core, block)


def placed(parts, hidden):
    return pl.pallas_call(
        place_kernel,
        name="placed",
        out_shape=(shape((M2, H), bf16), shape((16, 2 * F), f32), shape((16, 2 * H), f32)),
        in_specs=[VMEM] * 2,
        out_specs=[VMEM] * 3,
        compiler_params=limit(4),
    )(parts, hidden)


def flat(xh, core, xl, y, z):
    return ((((xh * 2 + core) * 2 + xl) * 4 + y) * 8) + z


def in_section(device, steps):
    return (device + steps * PEERS) % DEVICES


def other_core(device):
    return device ^ 64


def permuted(value, target):
    return lax.ppermute(value, ALL, [(device, target(device)) for device in range(DEVICES)])


DEV_GROUPS = [[section * PEERS + peer for peer in range(PEERS)] for section in range(4)]
PAIRS = (((0, 1), (2, 3)), ((0, 3), (1, 2)))


Z_PAIRS = (((0, 1), (3, 2), (4, 5), (7, 6)), ((0, 7), (1, 2), (4, 3), (5, 6)))
Z_PAIRS_LAST = (((0, 1), (2, 3), (4, 5), (6, 7)), ((0, 7), (1, 2), (4, 3), (5, 6)))


def cubes(stage):
    groups = []
    for core in range(2):
        side = core ^ stage
        for along_x in PAIRS[side]:
            for along_y in PAIRS[side]:
                for along_z in (Z_PAIRS, Z_PAIRS_LAST)[stage][side]:
                    groups.append([flat(x // 2, core, x % 2, y, z) for x in along_x for y in along_y for z in along_z])
    return groups


LAST_GROUPS = [
    [flat(section // 2, section % 2, xl, y, ring + z) for section in range(4) for z in (0, 4)]
    for xl in range(2)
    for y in range(4)
    for ring in range(4)
]


def exchanged(value, groups):
    return lax.all_to_all(value, ALL, 0, 0, axis_index_groups=groups, tiled=True)


def per_device(
    feature_store, send_rows, send_counts, target_one, neighbor_one, degree_one,
    target_two, neighbor_two, degree_two, weight_one, weight_two, cotangent,
):
    me = lax.axis_index(ALL).astype(jnp.int32).reshape(1)
    table = packed_table(neighbor_two, degree_two, target_two)
    table = permuted(table, lambda device: in_section(device, -1))
    cot = permuted(cotangent, lambda device: in_section(device, -1))

    outgoing = pick_rows(
        pltpu.with_memory_space_constraint(send_rows, pltpu.HBM),
        pltpu.with_memory_space_constraint(feature_store, pltpu.HBM),
    ).reshape(PEERS, CAP, F)
    arrived = exchanged(outgoing, DEV_GROUPS).reshape(TABLE, F)

    counts = count_matrix(neighbor_one, degree_one)
    joined, pre, hidden_two, grad_two, keep, send, w2 = forward(
        me, target_one, degree_one.reshape(4, 128), table, arrived, cot,
        *[pltpu.with_memory_space_constraint(value, pltpu.HBM) for value in (counts, weight_one, weight_two)],
    )
    theirs = permuted(grad_two, other_core)
    got = permuted(send, other_core)
    hidden_two = permuted(hidden_two, lambda device: in_section(device, 1))
    one = backward(table, grad_two, w2, pre, joined)
    parts = product(me, grad_two, theirs, keep, got, one)

    parts = summed_parts(exchanged(parts, cubes(0)))
    parts = spread_parts(exchanged(parts, cubes(1)).reshape(8, 2, 5, 16, 128))
    parts = exchanged(parts.reshape(8, 5, 16, 128), LAST_GROUPS).reshape(4, 2, 5, 16, 128)
    return placed(parts, hidden_two)


def solution(mesh):
    return jax.shard_map(
        per_device,
        mesh=mesh,
        in_specs=(
            P(ALL, None), P(ALL, None), P(ALL), P(ALL), P(None, ALL), P(ALL),
            P(ALL), P(None, ALL), P(ALL), P(), P(), P(ALL, None),
        ),
        out_specs=(P(ALL, None), P("dev", None), P("dev", None)),
        check_vma=False,
    )
```

```python
import jax
import jax.numpy as jnp
from jax import lax
from jax.experimental import pallas as pl
from jax.experimental.pallas import tpu as pltpu
from jax.sharding import PartitionSpec as P


F = 128
H = 1024
FAN1 = 15
FAN2 = 10
CAP = 64
STORE_ROWS = 4096
M2 = 128
M1 = 512
PEERS = 64
TABLE = PEERS * CAP
DEVICES = 256
ALL = ("sec", "dev")

bf16 = jnp.bfloat16
f32 = jnp.float32
VMEM = pl.BlockSpec(memory_space=pltpu.VMEM)
SMEM = pl.BlockSpec(memory_space=pltpu.SMEM)
HBM = pl.BlockSpec(memory_space=pltpu.HBM)


def limit(mib):
    return pltpu.CompilerParams(vmem_limit_bytes=mib * 1024 * 1024)


def shape(dims, dtype):
    return jax.ShapeDtypeStruct(dims, dtype)


def widen(source, wide, rows):
    def chunk(step, carry):
        here = pl.ds(pl.multiple_of(step * 256, 256), 256)
        wide[here, :] = source[here, :].astype(f32)
        return carry

    lax.fori_loop(0, rows // 256, chunk, 0)


def pick_kernel(rows_ref, store_ref, out_ref, wide, picked):
    widen(store_ref, wide, STORE_ROWS)

    for peer in range(PEERS):
        base = peer * CAP
        for slot in range(CAP):
            picked[base + slot : base + slot + 1, :] = wide[pl.ds(rows_ref[peer, slot], 1), :]
        out_ref[base : base + CAP, :] = picked[base : base + CAP, :].astype(bf16)


def pick_rows(send_rows, store):
    return pl.pallas_call(
        pick_kernel,
        name="pick_rows",
        out_shape=shape((TABLE, F), bf16),
        in_specs=[SMEM, VMEM],
        out_specs=VMEM,
        scratch_shapes=[pltpu.VMEM((STORE_ROWS, F), f32), pltpu.VMEM((TABLE, F), f32)],
        compiler_params=limit(10),
        cost_estimate=pl.CostEstimate(flops=0, bytes_accessed=2 << 20, transcendentals=0),
    )(send_rows, store)


def table_kernel(n2_ref, d2_ref, t2_ref, table_ref):
    table_ref[:FAN2, :] = n2_ref[...]
    table_ref[FAN2 : FAN2 + 1, :] = t2_ref[...]
    table_ref[FAN2 + 1 : FAN2 + 2, :] = d2_ref[...]
    table_ref[FAN2 + 2 :, :] = jnp.zeros((14 - FAN2, M2), jnp.int32)


def packed_table(n2, d2, t2):
    return pl.pallas_call(
        table_kernel,
        name="packed_table",
        out_shape=shape((16, M2), jnp.int32),
        in_specs=[VMEM] * 3,
        out_specs=VMEM,
        compiler_params=limit(2),
    )(n2, d2.reshape(1, M2), t2.reshape(1, M2))


def matrix_kernel(n1_ref, d1_ref, counts_ref, block, lane):
    order = lax.broadcasted_iota(jnp.int32, (FAN1, M1), 0)
    live = order < d1_ref[...]
    row = n1_ref[...]
    block[...] = jnp.where(live, row // 128, -1).astype(f32).T
    lane[...] = (row % 128).astype(f32).T
    lanes = lax.broadcasted_iota(jnp.int32, (16, 128), 1).astype(bf16)
    zero, one = jnp.zeros((16, 128), bf16), jnp.ones((16, 128), bf16)

    def sixteen_nodes(step, carry):
        rows = pl.ds(pl.multiple_of(step * 16, 16), 16)
        blocks = [jnp.broadcast_to(block[rows, k : k + 1], (16, 128)).astype(bf16) for k in range(FAN1)]
        hits = [
            jnp.where(jnp.broadcast_to(lane[rows, k : k + 1], (16, 128)).astype(bf16) == lanes, one, zero)
            for k in range(FAN1)
        ]
        for tile in range(TABLE // 128):
            columns = slice(tile * 128, tile * 128 + 128)
            terms = [jnp.where(blocks[k] == bf16(tile), hits[k], zero) for k in range(FAN1)]
            while len(terms) > 1:
                pairs = [a + b for a, b in zip(terms[::2], terms[1::2])]
                terms = pairs + ([terms[-1]] if len(terms) % 2 else [])
            counts_ref[rows, columns] = terms[0]
        return carry

    lax.fori_loop(0, M1 // 16, sixteen_nodes, 0)


def count_matrix(n1, d1):
    return pl.pallas_call(
        matrix_kernel,
        name="count_matrix",
        out_shape=shape((M1, TABLE), bf16),
        in_specs=[VMEM] * 2,
        out_specs=VMEM,
        scratch_shapes=[pltpu.VMEM((M1, FAN1), f32), pltpu.VMEM((M1, FAN1), f32)],
        compiler_params=limit(8),
        cost_estimate=pl.CostEstimate(flops=1 << 27, bytes_accessed=4 << 20, transcendentals=0),
    )(n1, d1.reshape(1, M1))


def as_column(row):
    return jnp.broadcast_to(row.astype(f32), (128, 128)).T


def slot_counts(table):
    places = lax.broadcasted_iota(jnp.int32, (M1, M2), 0)
    degree = table[11:12, :]
    counts = jnp.zeros((M1, M2), f32)
    for k in range(FAN2):
        live = (places == table[k : k + 1, :]) & (degree > k)
        counts = counts + live.astype(f32)
    chosen = (places == table[10:11, :]).astype(f32)
    return chosen.astype(bf16), counts.astype(bf16)


def over_rows(a, b):
    return lax.dot_general(a, b, (((0,), (0,)), ((), ())), preferred_element_type=f32)


def elu(v):
    return jnp.where(v > 0, v, jnp.exp(jnp.minimum(v, 0.0)) - 1.0)


def slope(v):
    return jnp.where(v > 0, 1.0, jnp.exp(jnp.minimum(v, 0.0)))


def forward_kernel(
    me_ref, targets_ref, degree_ref, table_ref, arrived_ref, cot_ref, counts_hbm, w1_hbm, w2_hbm,
    joined_ref, pre_ref, hidden_two_ref, grad_two_ref, keep_ref, send_ref, w2_ref,
    wide, chosen, hidden, counts_ref, w1_ref, counts_sem, w1_sem, w2_sem,
):
    loads = []
    for half in range(2):
        rows = pl.ds(half * M1 // 2, M1 // 2)
        loads.append(pltpu.make_async_copy(counts_hbm.at[rows], counts_ref.at[rows], counts_sem.at[half]))
    load_one = pltpu.make_async_copy(w1_hbm, w1_ref, w1_sem)
    load_two = pltpu.make_async_copy(w2_hbm, w2_ref, w2_sem)
    for load in loads + [load_one, load_two]:
        load.start()
    widen(arrived_ref, wide, TABLE)
    for node in range(M1):
        chosen[node : node + 1, :] = wide[pl.ds(targets_ref[node], 1), :]
    for half in range(2):
        rows = slice(half * M1 // 2, half * M1 // 2 + M1 // 2)
        loads[half].wait()
        summed = jnp.dot(counts_ref[rows, :], arrived_ref[...], preferred_element_type=f32)
        degree = jnp.concatenate([as_column(degree_ref[block : block + 1, :]) for block in (half * 2, half * 2 + 1)])
        joined_ref[rows, :F] = chosen[rows, :].astype(bf16)
        joined_ref[rows, F:] = (summed / degree).astype(bf16)
    load_one.wait()
    for block in range(M1 // 128):
        rows = slice(block * 128, block * 128 + 128)
        pre = jnp.dot(joined_ref[rows, :], w1_ref[...], preferred_element_type=f32)
        pre_ref[rows, :] = pre
        hidden[rows, :] = elu(pre).astype(bf16)

    table = table_ref[...]
    onehot, counts = slot_counts(table)
    own = over_rows(onehot, hidden[...]).astype(bf16)
    degree = as_column(table[11:12, :])
    mean = (over_rows(counts, hidden[...]) / jnp.tile(degree, (1, H // 128))).astype(bf16)
    load_two.wait()
    pre_two = jnp.dot(own, w2_ref[:H, :], preferred_element_type=f32) + jnp.dot(
        mean, w2_ref[H:, :], preferred_element_type=f32
    )
    hidden_two_ref[...] = elu(pre_two).astype(bf16)
    grad_two_ref[...] = (cot_ref[...].astype(f32) * slope(pre_two)).astype(bf16)
    first = me_ref[0] // PEERS % 2 == 0

    @pl.when(first)
    def _():
        keep_ref[...] = own
        send_ref[...] = mean

    @pl.when(jnp.logical_not(first))
    def _():
        keep_ref[...] = mean
        send_ref[...] = own


def forward(me, targets, degree, table, arrived, cot, counts, w1, w2):
    return pl.pallas_call(
        forward_kernel,
        name="forward",
        out_shape=(
            shape((M1, 2 * F), bf16),
            shape((M1, H), f32),
            shape((M2, H), bf16),
            shape((M2, H), bf16),
            shape((M2, H), bf16),
            shape((M2, H), bf16),
            shape((2 * H, H), bf16),
        ),
        in_specs=[SMEM, SMEM] + [VMEM] * 4 + [HBM] * 3,
        out_specs=[VMEM] * 7,
        scratch_shapes=[
            pltpu.VMEM((TABLE, F), f32),
            pltpu.VMEM((M1, F), f32),
            pltpu.VMEM((M1, H), bf16),
            pltpu.VMEM((M1, TABLE), bf16),
            pltpu.VMEM((2 * F, H), bf16),
            pltpu.SemaphoreType.DMA((2,)),
            pltpu.SemaphoreType.DMA,
            pltpu.SemaphoreType.DMA,
        ],
        compiler_params=limit(24),
        cost_estimate=pl.CostEstimate(flops=3 << 30, bytes_accessed=10 << 20, transcendentals=1 << 19),
    )(me, targets, degree, table, arrived, cot, counts, w1, w2)


def backward_kernel(table_ref, grad_two_ref, w2_ref, pre_ref, joined_ref, out_ref, stacked, spread, grad_pre):
    table = table_ref[...]
    grad_two = grad_two_ref[...]
    onehot, counts = slot_counts(table)
    stacked[:, :128] = onehot
    stacked[:, 128:256] = counts
    stacked[:, 256:] = counts
    dims = (((1,), (1,)), ((), ()))
    spread[:128, :] = lax.dot_general(grad_two, w2_ref[:H, :], dims, preferred_element_type=f32).astype(bf16)
    mean_grad = lax.dot_general(grad_two, w2_ref[H:, :], dims, preferred_element_type=f32).astype(bf16)
    degree = as_column(table[11:12, :])
    scaled = mean_grad.astype(f32) / jnp.tile(degree, (1, H // 128))
    high = scaled.astype(bf16)
    spread[128:256, :] = high
    spread[256:, :] = (scaled - high.astype(f32)).astype(bf16)
    for block in range(M1 // 128):
        rows = slice(block * 128, block * 128 + 128)
        grad_hidden = jnp.dot(stacked[rows, :], spread[...], preferred_element_type=f32).astype(bf16)
        grad_pre[rows, :] = (grad_hidden.astype(f32) * slope(pre_ref[rows, :])).astype(bf16)
    grad_one = over_rows(grad_pre[...], joined_ref[...]).astype(bf16)
    for xh in range(2):
        for rest in range(8):
            out_ref[xh * 8 + rest] = grad_one[rest * 128 : rest * 128 + 128, xh * 128 : xh * 128 + 128]


def backward(table, grad_two, w2, pre, joined):
    return pl.pallas_call(
        backward_kernel,
        name="backward",
        out_shape=shape((16, 128, 128), bf16),
        in_specs=[VMEM] * 5,
        out_specs=VMEM,
        scratch_shapes=[
            pltpu.VMEM((M1, 384), bf16),
            pltpu.VMEM((384, H), bf16),
            pltpu.VMEM((M1, H), bf16),
        ],
        compiler_params=limit(20),
        cost_estimate=pl.CostEstimate(flops=1 << 30, bytes_accessed=8 << 20, transcendentals=1 << 19),
    )(table, grad_two, w2, pre, joined)


def place_of(me, xh, xl, y):
    swapped = me // PEERS % 2 == 0

    def split(target, half):
        near, far = (target // 2 + target % 2 + half) % 2, target // 2
        return jnp.where(swapped, near, far), jnp.where(swapped, far, target % 2)

    outer_x, inner_x = split(xh * 2 + xl, me // 128)
    outer_y, inner_y = split(y, me // 16 % 2)
    return (outer_x * 2 + outer_y) * 2, (inner_x * 2 + inner_y) * 4, [split(ring, 0) for ring in range(4)]


def product_kernel(me_ref, mine_ref, theirs_ref, keep_ref, got_ref, one_ref, out_ref):
    for rest in range(8):
        rows = slice(rest * 128, rest * 128 + 128)
        product = over_rows(mine_ref[:, rows], keep_ref[...]) + over_rows(theirs_ref[:, rows], got_ref[...])
        product = product.astype(bf16)
        for xh in range(2):
            outer, inner, along_z = place_of(me_ref[0], xh, rest // 4, rest % 4)
            one = one_ref[xh * 8 + rest]
            for z in range(8):
                rows = slice(z * 16, z * 16 + 16)
                group = outer + along_z[z % 4][0]
                part = inner + along_z[z % 4][1] * 2 + z // 4
                for block in range(4):
                    column = (xh * 4 + block) * 128
                    out_ref[group, part, block] = product[rows, column : column + 128]
                out_ref[group, part, 4] = one[rows, :]


def product(me, mine, theirs, keep, got, one):
    return pl.pallas_call(
        product_kernel,
        name="product",
        out_shape=shape((8, 16, 5, 16, 128), bf16),
        in_specs=[SMEM] + [VMEM] * 5,
        out_specs=VMEM,
        compiler_params=limit(10),
        cost_estimate=pl.CostEstimate(flops=1 << 29, bytes_accessed=4 << 20, transcendentals=0),
    )(me, mine, theirs, keep, got, one)


def sum_kernel(parts_ref, out_ref):
    def total(first, count):
        if count == 1:
            return parts_ref[first].astype(f32)
        half = count // 2
        return total(first, half) + total(first + half, half)

    out_ref[...] = total(0, parts_ref.shape[0]).astype(out_ref.dtype)


def summed_parts(parts):
    return pl.pallas_call(
        sum_kernel,
        name="summed_parts",
        out_shape=shape(parts.shape[1:], bf16),
        in_specs=[VMEM],
        out_specs=VMEM,
        compiler_params=limit(8),
    )(parts)


def spread_kernel(parts_ref, out_ref, total):
    sum_kernel(parts_ref, total)
    for section in range(4):
        out_ref[section] = total[...]


def spread_parts(parts):
    return pl.pallas_call(
        spread_kernel,
        name="spread_parts",
        out_shape=shape((4,) + parts.shape[1:], bf16),
        in_specs=[VMEM],
        out_specs=VMEM,
        scratch_shapes=[pltpu.VMEM(parts.shape[1:], bf16)],
        compiler_params=limit(4),
    )(parts)


def place_kernel(parts_ref, hidden_ref, hidden_out, one_ref, two_ref):
    hidden_out[...] = hidden_ref[...]

    def piece(xh, core, block):
        section = xh * 2 + core
        return parts_ref[section, 0, block].astype(f32) + parts_ref[section, 1, block].astype(f32)

    for xh in range(2):
        one_ref[:, xh * F : xh * F + F] = piece(xh, 0, 4) + piece(xh, 1, 4)
        for core in range(2):
            for block in range(4):
                column = core * H + xh * 512 + block * 128
                two_ref[:, column : column + 128] = piece(xh, core, block)


def placed(parts, hidden):
    return pl.pallas_call(
        place_kernel,
        name="placed",
        out_shape=(shape((M2, H), bf16), shape((16, 2 * F), f32), shape((16, 2 * H), f32)),
        in_specs=[VMEM] * 2,
        out_specs=[VMEM] * 3,
        compiler_params=limit(4),
    )(parts, hidden)


def flat(xh, core, xl, y, z):
    return ((((xh * 2 + core) * 2 + xl) * 4 + y) * 8) + z


def in_section(device, steps):
    return (device + steps * PEERS) % DEVICES


def other_core(device):
    return device ^ 64


def permuted(value, target):
    return lax.ppermute(value, ALL, [(device, target(device)) for device in range(DEVICES)])


DEV_GROUPS = [[section * PEERS + peer for peer in range(PEERS)] for section in range(4)]
PAIRS = (((0, 1), (2, 3)), ((0, 3), (1, 2)))


Z_PAIRS = (((0, 1), (3, 2), (4, 5), (7, 6)), ((0, 7), (1, 2), (4, 3), (5, 6)))
Z_PAIRS_LAST = (((0, 1), (2, 3), (4, 5), (6, 7)), ((0, 7), (1, 2), (4, 3), (5, 6)))


def cubes(stage):
    groups = []
    for core in range(2):
        side = core ^ stage
        for along_x in PAIRS[side]:
            for along_y in PAIRS[side]:
                for along_z in (Z_PAIRS, Z_PAIRS_LAST)[stage][side]:
                    groups.append([flat(x // 2, core, x % 2, y, z) for x in along_x for y in along_y for z in along_z])
    return groups


LAST_GROUPS = [
    [flat(section // 2, section % 2, xl, y, ring + z) for section in range(4) for z in (0, 4)]
    for xl in range(2)
    for y in range(4)
    for ring in range(4)
]


def exchanged(value, groups):
    return lax.all_to_all(value, ALL, 0, 0, axis_index_groups=groups, tiled=True)


def per_device(
    feature_store, send_rows, send_counts, target_one, neighbor_one, degree_one,
    target_two, neighbor_two, degree_two, weight_one, weight_two, cotangent,
):
    me = lax.axis_index(ALL).astype(jnp.int32).reshape(1)
    table = packed_table(neighbor_two, degree_two, target_two)
    table = permuted(table, lambda device: in_section(device, -1))
    cot = permuted(cotangent, lambda device: in_section(device, -1))

    outgoing = pick_rows(
        pltpu.with_memory_space_constraint(send_rows, pltpu.HBM),
        pltpu.with_memory_space_constraint(feature_store, pltpu.HBM),
    ).reshape(PEERS, CAP, F)
    arrived = exchanged(outgoing, DEV_GROUPS).reshape(TABLE, F)

    counts = count_matrix(neighbor_one, degree_one)
    joined, pre, hidden_two, grad_two, keep, send, w2 = forward(
        me, target_one, degree_one.reshape(4, 128), table, arrived, cot,
        *[pltpu.with_memory_space_constraint(value, pltpu.HBM) for value in (counts, weight_one, weight_two)],
    )
    theirs = permuted(grad_two, other_core)
    got = permuted(send, other_core)
    hidden_two = permuted(hidden_two, lambda device: in_section(device, 1))
    one = backward(table, grad_two, w2, pre, joined)
    parts = product(me, grad_two, theirs, keep, got, one)

    parts, hidden_two = lax.optimization_barrier((exchanged(parts, cubes(0)), hidden_two))
    parts = summed_parts(parts)
    parts = spread_parts(exchanged(parts, cubes(1)).reshape(8, 2, 5, 16, 128))
    parts = exchanged(parts.reshape(8, 5, 16, 128), LAST_GROUPS).reshape(4, 2, 5, 16, 128)
    return placed(parts, hidden_two)


def solution(mesh):
    return jax.shard_map(
        per_device,
        mesh=mesh,
        in_specs=(
            P(ALL, None), P(ALL, None), P(ALL), P(ALL), P(None, ALL), P(ALL),
            P(ALL), P(None, ALL), P(ALL), P(), P(), P(ALL, None),
        ),
        out_specs=(P(ALL, None), P("dev", None), P("dev", None)),
        check_vma=False,
    )
```

```python
import functools

import jax
import jax.numpy as jnp
from jax import lax
from jax.experimental import pallas as pl
from jax.experimental.pallas import tpu as pltpu
from jax.sharding import PartitionSpec as P


F = 128
H = 1024
FAN1 = 15
FAN2 = 10
CAP = 64
STORE_ROWS = 4096
M2 = 128
M1 = 512
PEERS = 64
TABLE = PEERS * CAP
DEVICES = 256
ALL = ("sec", "dev")

bf16 = jnp.bfloat16
f32 = jnp.float32
VMEM = pl.BlockSpec(memory_space=pltpu.VMEM)
SMEM = pl.BlockSpec(memory_space=pltpu.SMEM)
HBM = pl.BlockSpec(memory_space=pltpu.HBM)


def limit(mib):
    return pltpu.CompilerParams(vmem_limit_bytes=mib * 1024 * 1024)


def shape(dims, dtype):
    return jax.ShapeDtypeStruct(dims, dtype)


def widen(source, wide, rows):
    def chunk(step, carry):
        here = pl.ds(pl.multiple_of(step * 256, 256), 256)
        wide[here, :] = source[here, :].astype(f32)
        return carry

    lax.fori_loop(0, rows // 256, chunk, 0)


def pick_kernel(rows_ref, store_ref, out_ref, wide, picked):
    widen(store_ref, wide, STORE_ROWS)

    for peer in range(PEERS):
        base = peer * CAP
        for slot in range(CAP):
            picked[base + slot : base + slot + 1, :] = wide[pl.ds(rows_ref[peer, slot], 1), :]
        out_ref[base : base + CAP, :] = picked[base : base + CAP, :].astype(bf16)


def pick_rows(send_rows, store):
    return pl.pallas_call(
        pick_kernel,
        name="pick_rows",
        out_shape=shape((TABLE, F), bf16),
        in_specs=[SMEM, VMEM],
        out_specs=VMEM,
        scratch_shapes=[pltpu.VMEM((STORE_ROWS, F), f32), pltpu.VMEM((TABLE, F), f32)],
        compiler_params=limit(10),
        cost_estimate=pl.CostEstimate(flops=0, bytes_accessed=2 << 20, transcendentals=0),
    )(send_rows, store)


def table_kernel(n2_ref, d2_ref, t2_ref, table_ref):
    table_ref[:FAN2, :] = n2_ref[...]
    table_ref[FAN2 : FAN2 + 1, :] = t2_ref[...]
    table_ref[FAN2 + 1 : FAN2 + 2, :] = d2_ref[...]
    table_ref[FAN2 + 2 :, :] = jnp.zeros((14 - FAN2, M2), jnp.int32)


def packed_table(n2, d2, t2):
    return pl.pallas_call(
        table_kernel,
        name="packed_table",
        out_shape=shape((16, M2), jnp.int32),
        in_specs=[VMEM] * 3,
        out_specs=VMEM,
        compiler_params=limit(2),
    )(n2, d2.reshape(1, M2), t2.reshape(1, M2))


def matrix_kernel(n1_ref, d1_ref, counts_ref, block, lane):
    order = lax.broadcasted_iota(jnp.int32, (FAN1, M1), 0)
    live = order < d1_ref[...]
    row = n1_ref[...]
    block[...] = jnp.where(live, row // 128, -1).astype(f32).T
    lane[...] = (row % 128).astype(f32).T
    lanes = lax.broadcasted_iota(jnp.int32, (16, 128), 1).astype(bf16)
    zero, one = jnp.zeros((16, 128), bf16), jnp.ones((16, 128), bf16)

    def sixteen_nodes(step, carry):
        rows = pl.ds(pl.multiple_of(step * 16, 16), 16)
        blocks = [jnp.broadcast_to(block[rows, k : k + 1], (16, 128)).astype(bf16) for k in range(FAN1)]
        hits = [
            jnp.where(jnp.broadcast_to(lane[rows, k : k + 1], (16, 128)).astype(bf16) == lanes, one, zero)
            for k in range(FAN1)
        ]
        for tile in range(TABLE // 128):
            columns = slice(tile * 128, tile * 128 + 128)
            terms = [jnp.where(blocks[k] == bf16(tile), hits[k], zero) for k in range(FAN1)]
            while len(terms) > 1:
                pairs = [a + b for a, b in zip(terms[::2], terms[1::2])]
                terms = pairs + ([terms[-1]] if len(terms) % 2 else [])
            counts_ref[rows, columns] = terms[0]
        return carry

    lax.fori_loop(0, M1 // 16, sixteen_nodes, 0)


def count_matrix(n1, d1):
    return pl.pallas_call(
        matrix_kernel,
        name="count_matrix",
        out_shape=shape((M1, TABLE), bf16),
        in_specs=[VMEM] * 2,
        out_specs=VMEM,
        scratch_shapes=[pltpu.VMEM((M1, FAN1), f32), pltpu.VMEM((M1, FAN1), f32)],
        compiler_params=limit(8),
        cost_estimate=pl.CostEstimate(flops=1 << 27, bytes_accessed=4 << 20, transcendentals=0),
    )(n1, d1.reshape(1, M1))


def as_column(row):
    return jnp.broadcast_to(row.astype(f32), (128, 128)).T


def slot_counts(table):
    places = lax.broadcasted_iota(jnp.int32, (M1, M2), 0)
    degree = table[11:12, :]
    counts = jnp.zeros((M1, M2), f32)
    for k in range(FAN2):
        live = (places == table[k : k + 1, :]) & (degree > k)
        counts = counts + live.astype(f32)
    chosen = (places == table[10:11, :]).astype(f32)
    return chosen.astype(bf16), counts.astype(bf16)


def over_rows(a, b):
    return lax.dot_general(a, b, (((0,), (0,)), ((), ())), preferred_element_type=f32)


def elu(v):
    return jnp.where(v > 0, v, jnp.exp(jnp.minimum(v, 0.0)) - 1.0)


def slope(v):
    return jnp.where(v > 0, 1.0, jnp.exp(jnp.minimum(v, 0.0)))


def forward_kernel(
    me_ref, targets_ref, degree_ref, table_ref, arrived_ref, cot_ref, counts_hbm, w1_hbm, w2_hbm,
    joined_ref, pre_ref, hidden_two_ref, grad_two_ref, keep_ref, send_ref, w2_ref,
    wide, chosen, hidden, counts_ref, w1_ref, counts_sem, w1_sem, w2_sem,
):
    loads = []
    for half in range(2):
        rows = pl.ds(half * M1 // 2, M1 // 2)
        loads.append(pltpu.make_async_copy(counts_hbm.at[rows], counts_ref.at[rows], counts_sem.at[half]))
    load_one = pltpu.make_async_copy(w1_hbm, w1_ref, w1_sem)
    load_two = pltpu.make_async_copy(w2_hbm, w2_ref, w2_sem)
    for load in loads + [load_one, load_two]:
        load.start()
    widen(arrived_ref, wide, TABLE)
    for node in range(M1):
        chosen[node : node + 1, :] = wide[pl.ds(targets_ref[node], 1), :]
    for half in range(2):
        rows = slice(half * M1 // 2, half * M1 // 2 + M1 // 2)
        loads[half].wait()
        summed = jnp.dot(counts_ref[rows, :], arrived_ref[...], preferred_element_type=f32)
        degree = jnp.concatenate([as_column(degree_ref[block : block + 1, :]) for block in (half * 2, half * 2 + 1)])
        joined_ref[rows, :F] = chosen[rows, :].astype(bf16)
        joined_ref[rows, F:] = (summed / degree).astype(bf16)
    load_one.wait()
    for block in range(M1 // 128):
        rows = slice(block * 128, block * 128 + 128)
        pre = jnp.dot(joined_ref[rows, :], w1_ref[...], preferred_element_type=f32)
        pre_ref[rows, :] = pre
        hidden[rows, :] = elu(pre).astype(bf16)

    table = table_ref[...]
    onehot, counts = slot_counts(table)
    own = over_rows(onehot, hidden[...]).astype(bf16)
    degree = as_column(table[11:12, :])
    mean = (over_rows(counts, hidden[...]) / jnp.tile(degree, (1, H // 128))).astype(bf16)
    load_two.wait()
    pre_two = jnp.dot(own, w2_ref[:H, :], preferred_element_type=f32) + jnp.dot(
        mean, w2_ref[H:, :], preferred_element_type=f32
    )
    hidden_two_ref[...] = elu(pre_two).astype(bf16)
    grad_two_ref[...] = (cot_ref[...].astype(f32) * slope(pre_two)).astype(bf16)
    first = me_ref[0] // PEERS % 2 == 0

    @pl.when(first)
    def _():
        keep_ref[...] = own
        send_ref[...] = mean

    @pl.when(jnp.logical_not(first))
    def _():
        keep_ref[...] = mean
        send_ref[...] = own


def forward(me, targets, degree, table, arrived, cot, counts, w1, w2):
    return pl.pallas_call(
        forward_kernel,
        name="forward",
        out_shape=(
            shape((M1, 2 * F), bf16),
            shape((M1, H), f32),
            shape((M2, H), bf16),
            shape((M2, H), bf16),
            shape((M2, H), bf16),
            shape((M2, H), bf16),
            shape((2 * H, H), bf16),
        ),
        in_specs=[SMEM, SMEM] + [VMEM] * 4 + [HBM] * 3,
        out_specs=[VMEM] * 7,
        scratch_shapes=[
            pltpu.VMEM((TABLE, F), f32),
            pltpu.VMEM((M1, F), f32),
            pltpu.VMEM((M1, H), bf16),
            pltpu.VMEM((M1, TABLE), bf16),
            pltpu.VMEM((2 * F, H), bf16),
            pltpu.SemaphoreType.DMA((2,)),
            pltpu.SemaphoreType.DMA,
            pltpu.SemaphoreType.DMA,
        ],
        compiler_params=limit(24),
        cost_estimate=pl.CostEstimate(flops=3 << 30, bytes_accessed=10 << 20, transcendentals=1 << 19),
    )(me, targets, degree, table, arrived, cot, counts, w1, w2)


def backward_kernel(table_ref, grad_two_ref, w2_ref, pre_ref, joined_ref, out_ref, stacked, spread, grad_pre):
    table = table_ref[...]
    grad_two = grad_two_ref[...]
    onehot, counts = slot_counts(table)
    stacked[:, :128] = onehot
    stacked[:, 128:256] = counts
    stacked[:, 256:] = counts
    dims = (((1,), (1,)), ((), ()))
    spread[:128, :] = lax.dot_general(grad_two, w2_ref[:H, :], dims, preferred_element_type=f32).astype(bf16)
    mean_grad = lax.dot_general(grad_two, w2_ref[H:, :], dims, preferred_element_type=f32).astype(bf16)
    degree = as_column(table[11:12, :])
    scaled = mean_grad.astype(f32) / jnp.tile(degree, (1, H // 128))
    high = scaled.astype(bf16)
    spread[128:256, :] = high
    spread[256:, :] = (scaled - high.astype(f32)).astype(bf16)
    for block in range(M1 // 128):
        rows = slice(block * 128, block * 128 + 128)
        grad_hidden = jnp.dot(stacked[rows, :], spread[...], preferred_element_type=f32).astype(bf16)
        grad_pre[rows, :] = (grad_hidden.astype(f32) * slope(pre_ref[rows, :])).astype(bf16)
    grad_one = over_rows(grad_pre[...], joined_ref[...]).astype(bf16)
    for xh in range(2):
        for rest in range(8):
            out_ref[xh * 8 + rest] = grad_one[rest * 128 : rest * 128 + 128, xh * 128 : xh * 128 + 128]


def backward(table, grad_two, w2, pre, joined):
    return pl.pallas_call(
        backward_kernel,
        name="backward",
        out_shape=shape((16, 128, 128), bf16),
        in_specs=[VMEM] * 5,
        out_specs=VMEM,
        scratch_shapes=[
            pltpu.VMEM((M1, 384), bf16),
            pltpu.VMEM((384, H), bf16),
            pltpu.VMEM((M1, H), bf16),
        ],
        compiler_params=limit(20),
        cost_estimate=pl.CostEstimate(flops=1 << 30, bytes_accessed=8 << 20, transcendentals=1 << 19),
    )(table, grad_two, w2, pre, joined)


def place_of(me, xh, xl, y):
    swapped = me // PEERS % 2 == 0

    def split(target, half):
        near, far = (target // 2 + target % 2 + half) % 2, target // 2
        return jnp.where(swapped, near, far), jnp.where(swapped, far, target % 2)

    outer_x, inner_x = split(xh * 2 + xl, me // 128)
    outer_y, inner_y = split(y, me // 16 % 2)
    return (outer_x * 2 + outer_y) * 2, (inner_x * 2 + inner_y) * 4


def product_kernel(me_ref, mine_ref, theirs_ref, keep_ref, got_ref, one_ref, out_ref):
    me = me_ref[0]
    home = place_of(me, me // 128, me // 32 % 2, me // 8 % 4)[0] + me % 2
    for rest in range(8):
        rows = slice(rest * 128, rest * 128 + 128)
        product = over_rows(mine_ref[:, rows], keep_ref[...]) + over_rows(theirs_ref[:, rows], got_ref[...])
        product = product.astype(bf16)
        for xh in range(2):
            outer, inner = place_of(me, xh, rest // 4, rest % 4)
            one = one_ref[xh * 8 + rest]
            for z in range(8):
                rows = slice(z * 16, z * 16 + 16)
                for block in range(4):
                    column = (xh * 4 + block) * 128
                    out_ref[(outer + z % 2) ^ home, inner + z // 2, block] = product[rows, column : column + 128]
                out_ref[(outer + z % 2) ^ home, inner + z // 2, 4] = one[rows, :]


def product(me, mine, theirs, keep, got, one):
    return pl.pallas_call(
        product_kernel,
        name="product",
        out_shape=shape((8, 16, 5, 16, 128), bf16),
        in_specs=[SMEM] + [VMEM] * 5,
        out_specs=VMEM,
        compiler_params=limit(10),
        cost_estimate=pl.CostEstimate(flops=1 << 29, bytes_accessed=4 << 20, transcendentals=0),
    )(me, mine, theirs, keep, got, one)


def sum_kernel(parts_ref, out_ref):
    def total(first, count):
        if count == 1:
            return parts_ref[first].astype(f32)
        half = count // 2
        return total(first, half) + total(first + half, half)

    out_ref[...] = total(0, parts_ref.shape[0]).astype(out_ref.dtype)


def summed_parts(parts, dtype):
    return pl.pallas_call(
        sum_kernel,
        name="summed_parts",
        out_shape=shape(parts.shape[1:], dtype),
        in_specs=[VMEM],
        out_specs=VMEM,
        compiler_params=limit(8),
    )(parts)


def arrived_kernel(parts_ref, *refs):
    *others, out_ref = refs
    terms = [parts_ref[0].astype(f32)] + [other[...].astype(f32) for other in others]
    while len(terms) > 1:
        terms = [a + b for a, b in zip(terms[::2], terms[1::2])]
    out_ref[...] = terms[0].astype(bf16)


def summed_arrivals(parts, others):
    return pl.pallas_call(
        arrived_kernel,
        name="summed_arrivals",
        out_shape=shape(parts.shape[1:], bf16),
        in_specs=[VMEM] * 8,
        out_specs=VMEM,
        compiler_params=limit(8),
    )(parts, *others)


def place_kernel(me_ref, mine_ref, core_ref, xh_ref, both_ref, hidden_ref, hidden_out, one_ref, two_ref):
    hidden_out[...] = hidden_ref[...]
    my_xh, my_core = me_ref[0] // 128, me_ref[0] // PEERS % 2

    def piece(xh, core, block):
        same = jnp.where(my_core == core, mine_ref[block], core_ref[block])
        other = jnp.where(my_core == core, xh_ref[block], both_ref[block])
        return jnp.where(my_xh == xh, same, other)

    for xh in range(2):
        one_ref[:, xh * F : xh * F + F] = piece(xh, 0, 4) + piece(xh, 1, 4)
        for core in range(2):
            for block in range(4):
                column = core * H + xh * 512 + block * 128
                two_ref[:, column : column + 128] = piece(xh, core, block)


def placed(me, mine, core, xh, both, hidden):
    return pl.pallas_call(
        place_kernel,
        name="placed",
        out_shape=(shape((M2, H), bf16), shape((16, 2 * F), f32), shape((16, 2 * H), f32)),
        in_specs=[SMEM] + [VMEM] * 5,
        out_specs=[VMEM] * 3,
        compiler_params=limit(4),
    )(me, mine, core, xh, both, hidden)


def flat(xh, core, xl, y, z):
    return ((((xh * 2 + core) * 2 + xl) * 4 + y) * 8) + z


def in_section(device, steps):
    return (device + steps * PEERS) % DEVICES


def other_core(device):
    return device ^ 64


def other_xh(device):
    return device ^ 128


def permuted(value, target):
    return lax.ppermute(value, ALL, [(device, target(device)) for device in range(DEVICES)])


DEV_GROUPS = [[section * PEERS + peer for peer in range(PEERS)] for section in range(4)]
PAIRS = (((0, 1), (2, 3)), ((0, 3), (1, 2)))


def cube_partner(device, way):
    xh, core, xl, y, z = device // 128, device // 64 % 2, device // 32 % 2, device // 8 % 4, device % 8
    x = xh * 2 + xl
    if way & 4:
        x = 3 - x if core else x ^ 1
    if way & 2:
        y = 3 - y if core else y ^ 1
    if way & 1:
        z = (z + (1 if z % 2 else -1)) % 8 if core else z ^ 1
    return flat(x // 2, core, x % 2, y, z)


def rests():
    groups = []
    for core in range(2):
        for along_x in PAIRS[1 - core]:
            for along_y in PAIRS[1 - core]:
                for parity in range(2):
                    along_z = range(parity, 8, 2)
                    groups.append([flat(x // 2, core, x % 2, y, z) for x in along_x for y in along_y for z in along_z])
    return groups


def exchanged(value, groups):
    return lax.all_to_all(value, ALL, 0, 0, axis_index_groups=groups, tiled=True)


def per_device(
    feature_store, send_rows, send_counts, target_one, neighbor_one, degree_one,
    target_two, neighbor_two, degree_two, weight_one, weight_two, cotangent,
):
    me = lax.axis_index(ALL).astype(jnp.int32).reshape(1)
    table = packed_table(neighbor_two, degree_two, target_two)
    table = permuted(table, lambda device: in_section(device, -1))
    cot = permuted(cotangent, lambda device: in_section(device, -1))

    outgoing = pick_rows(
        pltpu.with_memory_space_constraint(send_rows, pltpu.HBM),
        pltpu.with_memory_space_constraint(feature_store, pltpu.HBM),
    ).reshape(PEERS, CAP, F)
    arrived = exchanged(outgoing, DEV_GROUPS).reshape(TABLE, F)

    counts = count_matrix(neighbor_one, degree_one)
    joined, pre, hidden_two, grad_two, keep, send, w2 = forward(
        me, target_one, degree_one.reshape(4, 128), table, arrived, cot,
        *[pltpu.with_memory_space_constraint(value, pltpu.HBM) for value in (counts, weight_one, weight_two)],
    )
    theirs = permuted(grad_two, other_core)
    got = permuted(send, other_core)
    hidden_two = permuted(hidden_two, lambda device: in_section(device, 1))
    one = backward(table, grad_two, w2, pre, joined)
    parts = product(me, grad_two, theirs, keep, got, one)

    others = [permuted(parts[way], functools.partial(cube_partner, way=way)) for way in (7, 6, 5, 3, 4, 2, 1)]
    parts = summed_arrivals(parts, others)
    mine = summed_parts(exchanged(parts, rests()), f32)
    from_core = permuted(mine, other_core)
    from_xh = permuted(mine, other_xh)
    from_both = permuted(from_core, other_xh)
    return placed(me, mine, from_core, from_xh, from_both, hidden_two)


def solution(mesh):
    return jax.shard_map(
        per_device,
        mesh=mesh,
        in_specs=(
            P(ALL, None), P(ALL, None), P(ALL), P(ALL), P(None, ALL), P(ALL),
            P(ALL), P(None, ALL), P(ALL), P(), P(), P(ALL, None),
        ),
        out_specs=(P(ALL, None), P("dev", None), P("dev", None)),
        check_vma=False,
    )
```
